128 devices in a mesh: lat: 8 (over z, core), lon: 16 (over x, y).
Axes of the slice: x: 4, y: 4, z: 4, core: 2. Of those that a mesh axis runs over, the one named last changes fastest.
Arguments:
- adjoint_state: float32 [2, 72, 128, 2048], P(None, None, 'lat', 'lon'), may hold values from -6 to 6
- courant_east: float32 [72, 128, 2048], P(None, 'lat', 'lon'), may hold values from -0.45 to 0.45
- courant_north: float32 [72, 128, 2048], P(None, 'lat', 'lon'), may hold values from -0.45 to 0.45
- diffusion: float32 [128, 2048], P('lat', 'lon'), may hold values from 0.05 to 0.45
- convective_flux: float32 [128, 2048], P('lat', 'lon'), may hold values from 0.1 to 1
- convection: float32 [72, 72], replicated, may hold values from -0.75 to 0.75
- sounding_forcing: bfloat16 [786432, 128], P(('lat', 'lon')), may hold values from -6 to 6
- sounding_column: int32 [786432], P(('lat', 'lon')), may hold values from 0 to 2047
- sounding_level: int32 [786432], P(('lat', 'lon')), may hold values from 0 to 8
- owner_counts: int32 [128, 128], P(('lat', 'lon')), may hold values from 8 to 48, as said below
Outputs:
- adjoint_final: float32 [2, 72, 128, 2048], P(None, None, 'lat', 'lon')
- flux_gradient: float32 [2, 128, 2048], P(None, 'lat', 'lon')
The draws below stay inside these ranges and needn't reach their ends.
Inputs may be any that keep to these rules, and one draw needn't show every extreme that they name: `owner_counts`: each owner gets max(1, 8) to 48 rows of every device's list; every device sends exactly 48 to one owner, the same owner for all devices; the blocks stand in order of owner from row 0, and rows past the device's total are unused.
All inputs are finite; a program needn't handle non-finite values.
Results may differ from the reference program's by a relative error of at most 0.0003.
Values may be sent and summed in bfloat16 or wider, within the bound.
A program may use at most 64 MiB of HBM per device.

```python
import math
import jax
import jax.numpy as jnp
from jax import lax

TR = 2
LEV = 72
SPAN = 64
CAP = 48
CLAT = 16
CLON = 128
NDEV = 128
CELLS = 2048
NLAT = 128
NLON = 2048
SND_DEV = 6144
NSND = 786432
N_LON = 16


def draw_owner_counts(key, part):
    first_key, second_key, third_key = jax.random.split(key, 3)
    lowest = max(1, CAP // 6)
    first = jax.random.randint(first_key, (NDEV, NDEV), 0, 8)
    second = jax.random.randint(second_key, (NDEV, NDEV), 0, 8)
    counts = jnp.minimum(lowest + first * second, CAP)
    chosen = jax.random.randint(third_key, (), 0, NDEV)
    columns = jnp.arange(NDEV)[None, :]
    rows = jnp.arange(NDEV)[:, None]
    counts = jnp.where((rows == 0) & (columns == (chosen + 1) % NDEV), lowest, counts)
    counts = jnp.where(columns == chosen, CAP, counts)
    return counts.astype(jnp.int32)


def place_ends(values, rng, smallest, largest):
    longest = values.shape.index(max(values.shape))
    spots = []
    for shift in (0, 1):
        where = [jax.random.randint(jax.random.fold_in(rng, axis), (), 0, length) for axis, length in enumerate(values.shape)]
        where[longest] = (where[longest] + shift) % values.shape[longest]
        spots.append(tuple(where))
    return values.at[spots[0]].set(smallest).at[spots[1]].set(largest)


def steps_of(stream_key, dims, pieces, low, high):
    def one(position, shards_of):
        steps = jax.random.uniform(jax.random.fold_in(jax.random.fold_in(stream_key, 6), position), (shards_of,), jnp.float32, low / len(pieces), high / len(pieces))
        return jnp.repeat(jnp.exp(steps), dims[position] // shards_of).reshape((-1,) + (1,) * (len(dims) - position - 1))

    level = one(*pieces[0])
    for cut in pieces[1:]:
        level = level * one(*cut)
    return level


def normal_values(rng, extent, deviation, bound, cuts=(), kind=jnp.bfloat16):
    values = deviation * jax.random.normal(rng, extent, jnp.float32)
    if cuts:
        values = values * steps_of(rng, extent, cuts, -0.22, 0.18)
    return jnp.clip(values, -bound, bound).astype(kind)


def setup_inputs(seed: int = 0) -> dict:
    key_of = jax.random.split(jax.random.key(seed), 11)
    return {
        "adjoint_state": normal_values(key_of[0], (TR, LEV, NLAT, NLON), 1.0, 6.0, ((2, 8), (3, 16)), jnp.float32),
        "courant_east": jnp.clip(jax.random.uniform(key_of[1], (LEV, NLAT, NLON), jnp.float32, -0.45, 0.45) * steps_of(key_of[1], (LEV, NLAT, NLON), ((1, 8), (2, 16)), -0.4, 0.0), -0.45, 0.45),
        "courant_north": jnp.clip(jax.random.uniform(key_of[2], (LEV, NLAT, NLON), jnp.float32, -0.45, 0.45) * steps_of(key_of[2], (LEV, NLAT, NLON), ((1, 8), (2, 16)), -0.4, 0.0), -0.45, 0.45),
        "diffusion": jnp.clip(jnp.exp(math.log(0.45) - 2.1972245 * jax.random.uniform(key_of[3], (NLAT, NLON), jnp.float32) ** steps_of(key_of[3], (NLAT, NLON), ((0, 8), (1, 16)), -0.2, 0.2)), 0.05, 0.45),
        "convective_flux": jnp.clip(jnp.exp(math.log(1.0) - 2.3025851 * jax.random.uniform(key_of[4], (NLAT, NLON), jnp.float32) ** steps_of(key_of[4], (NLAT, NLON), ((0, 8), (1, 16)), -0.2, 0.2)), 0.1, 1.0),
        "convection": normal_values(key_of[5], (LEV, LEV), LEV ** -0.5, 0.75, (), jnp.float32),
        "sounding_forcing": normal_values(key_of[6], (NSND, TR * SPAN), 1.0, 6.0, ((0, 128),)),
        "sounding_column": place_ends(jax.random.randint(key_of[7], (NSND,), 0, CELLS), jax.random.fold_in(key_of[7], 1), 0, CELLS - 1).astype(jnp.int32),
        "sounding_level": place_ends(jax.random.randint(key_of[8], (NSND,), 0, LEV - SPAN + 1), jax.random.fold_in(key_of[8], 1), 0, LEV - SPAN).astype(jnp.int32),
        "owner_counts": draw_owner_counts(jax.random.fold_in(key_of[10], 71), 0),
    }


def column_physics(state, convection, diffusion, convective_flux):
    flat = state.reshape(TR, LEV, NLAT * NLON)
    mixed = jnp.einsum("lk,tlc->tkc", convection, flat, precision=lax.Precision.HIGHEST)
    mixed = flat + convective_flux.reshape(1, 1, -1) * mixed
    above = jnp.concatenate([mixed[:, 1:], mixed[:, -1:]], axis=1)
    below = jnp.concatenate([mixed[:, :1], mixed[:, :-1]], axis=1)
    mixed = mixed + diffusion.reshape(1, 1, -1) * (above - 2.0 * mixed + below)
    return mixed.reshape(TR, LEV, NLAT, NLON)


def advect(field, courant_east, courant_north):
    zero_row = jnp.zeros_like(field[:, :, :1])
    east = jnp.roll(field, -1, axis=3)
    west = jnp.roll(field, 1, axis=3)
    north = jnp.concatenate([field[:, :, 1:], zero_row], axis=2)
    south = jnp.concatenate([zero_row, field[:, :, :-1]], axis=2)
    rows = jnp.arange(NLAT, dtype=jnp.int32)[None, :, None]
    north_face = jnp.where(rows == NLAT - 1, jnp.zeros_like(courant_north), courant_north)
    south_face = jnp.concatenate([jnp.zeros_like(courant_north[:, :1]), courant_north[:, :-1]], axis=1)
    west_face = jnp.roll(courant_east, 1, axis=2)
    result = field + jnp.maximum(courant_east, 0.0) * (east - field)
    result = result + jnp.minimum(west_face, 0.0) * (field - west)
    result = result + jnp.maximum(north_face, 0.0) * (north - field)
    result = result + jnp.minimum(south_face, 0.0) * (field - south)
    return result


def sounding_field(sounding_forcing, sounding_column, sounding_level, owner_counts):
    blocks_all = sounding_forcing.reshape(NDEV, SND_DEV, TR, SPAN)
    columns_all = sounding_column.reshape(NDEV, SND_DEV)
    levels_all = sounding_level.reshape(NDEV, SND_DEV)

    def add_source(field, items):
        blocks, columns, levels, row_counts = items
        ends = jnp.cumsum(row_counts).astype(jnp.int32)
        row_ids = jnp.arange(SND_DEV, dtype=jnp.int32)
        owner = jnp.sum((row_ids[:, None] >= ends[None, :]).astype(jnp.int32), axis=1).astype(jnp.int32)
        valid = row_ids < ends[-1]
        owner = jnp.minimum(owner, NDEV - 1)
        glat = (owner // N_LON) * CLAT + columns // CLON
        glon = (owner % N_LON) * CLON + columns % CLON
        target = (glat * NLON + glon).astype(jnp.int32)
        offset = jnp.arange(LEV, dtype=jnp.int32)[:, None] - levels[None, :]
        inside = (offset >= 0) & (offset < SPAN) & valid[None, :]
        arranged = jnp.transpose(blocks, (1, 2, 0)).astype(jnp.float32)
        index = jnp.broadcast_to(jnp.clip(offset, 0, SPAN - 1)[None], (TR, LEV, SND_DEV))
        placed = jnp.take_along_axis(arranged, index, axis=1)
        placed = jnp.where(inside[None], placed, jnp.zeros_like(placed))
        return field.at[:, :, target].add(placed), None

    start = jnp.zeros((TR, LEV, NLAT * NLON), jnp.float32)
    field, unused = lax.scan(add_source, start, (blocks_all, columns_all, levels_all, owner_counts))
    return field.reshape(TR, LEV, NLAT, NLON)


def reference(adjoint_state, courant_east, courant_north, diffusion, convective_flux, convection, sounding_forcing, sounding_column, sounding_level, owner_counts):
    first = advect(column_physics(adjoint_state, convection, diffusion, convective_flux), courant_east, courant_north)
    forced = first + sounding_field(sounding_forcing, sounding_column, sounding_level, owner_counts)
    second = advect(column_physics(forced, convection, diffusion, convective_flux), courant_east, courant_north)
    return second, forced[:, 0] + second[:, 0]
```

```python
import jax
import jax.numpy as jnp
from jax import lax
from jax.experimental import pallas as pl
from jax.experimental.pallas import tpu as pltpu
from jax.sharding import PartitionSpec as P

TR = 2
LEV = 72
SPAN = 64
CAP = 48
CLAT = 16
LANES = 128
CHIPS = 64
STRIDE = 45
BLOCK = 2 * CAP + 16
GROUP = 16
GROUPS = CHIPS // GROUP
ROWS = GROUP * CAP
F32 = jnp.float32
BF16 = jnp.bfloat16
MESH = pl.DeviceIdType.MESH


def place():
    lat = lax.axis_index("lat")
    lon = lax.axis_index("lon")
    return lat, lon, lax.rem(lat, 2), (lat // 2) * 16 + lon


def peer_chip(chip, step):
    return jnp.bitwise_xor(chip, lax.rem(step * STRIDE, CHIPS))


def iota(shape, axis):
    return lax.broadcasted_iota(jnp.int32, shape, axis)


def pack_kernel(counts, forcing, column, level, out, rows_f32, codes, starts):
    lat, lon, core, chip = place()

    def prefix(o, total):
        starts[o] = total
        return total + counts[0, o]

    lax.fori_loop(0, 128, prefix, jnp.int32(0))

    def widen(i, carry):
        at = pl.ds(pl.multiple_of(i * 256, 256), 256)
        rows_f32[at, :] = forcing[at, :].astype(F32)
        return carry

    lax.fori_loop(0, forcing.shape[0] // 256, widen, 0)
    codes[0:48, :] = level[...] * 2048 + column[...]
    codes[48:56, :] = jnp.zeros((8, LANES), jnp.int32)
    lane = iota((8, LANES), 1)
    sub = iota((16, LANES), 0)

    def step(i, carry):
        t = peer_chip(chip, i)
        first_lane = lax.rem(i * CAP, LANES)
        slot = jnp.bitwise_and(lane - first_lane, LANES - 1)
        tile = jnp.zeros((16, LANES), F32)
        for dc in range(2):
            owner = ((t // 16) * 2 + dc) * 16 + lax.rem(t, 16)
            start = starts[owner]
            count = counts[0, owner]
            out[i, dc * CAP : (dc + 1) * CAP, :] = rows_f32[pl.ds(start, CAP), :].astype(BF16)
            row = start // LANES
            off = lax.rem(start, LANES)
            turn = lax.rem(first_lane - off + LANES, LANES)
            near = pltpu.roll(jnp.broadcast_to(codes[pl.ds(row, 1), :], (8, LANES)), turn, 1)
            far = pltpu.roll(jnp.broadcast_to(codes[pl.ds(row + 1, 1), :], (8, LANES)), turn, 1)
            code = jnp.where(slot < LANES - off, near, far)
            valid = slot < count
            shift = jnp.where(valid, jnp.right_shift(code, 11), 0)
            lat_row = jnp.where(valid, jnp.bitwise_and(jnp.right_shift(code, 7), 15), -1)
            lon_col = jnp.bitwise_and(code, 127)
            for k, part in enumerate((shift, lat_row, lon_col)):
                part = part.astype(F32)
                both = jnp.concatenate([part, part], axis=0)
                tile = jnp.where(sub == dc * 3 + k, both, tile)
        out[i, 2 * CAP : BLOCK, :] = tile.astype(BF16)
        return carry

    lax.fori_loop(0, CHIPS, step, 0)


def pack(counts, forcing, column, level):
    vmem = pl.BlockSpec(memory_space=pltpu.VMEM)
    return pl.pallas_call(
        pack_kernel,
        out_shape=jax.ShapeDtypeStruct((CHIPS, BLOCK, LANES), BF16),
        in_specs=[pl.BlockSpec(memory_space=pltpu.SMEM), vmem, vmem, vmem],
        out_specs=vmem,
        scratch_shapes=[
            pltpu.VMEM((forcing.shape[0], LANES), F32),
            pltpu.VMEM((56, LANES), jnp.int32),
            pltpu.SMEM((128,), jnp.int32),
        ],
        compiler_params=pltpu.CompilerParams(vmem_limit_bytes=24 << 20),
        name="pack",
    )(counts, forcing, column.reshape(48, LANES), level.reshape(48, LANES))


def main_kernel(
    adj, ce, cn, dif, flx, conv, send,
    out, flux,
    recv, fwd, fwdc, acc, field, gains, mixer, codes, edges, west_in, east_in, cn_edge, cn_south,
    send_sem, recv_sem, fwd_send, fwd_recv, halo_send, halo_recv, self_sem,
):
    lat, lon, core, chip = place()
    north = lax.rem(lat + 1, 8)
    south = lax.rem(lat + 7, 8)
    east = lax.rem(lon + 1, 16)
    west = lax.rem(lon + 15, 16)
    sibling = lat + 1 - 2 * core
    barrier = pltpu.get_barrier_semaphore()

    def peer(i):
        t = peer_chip(chip, i)
        return ((t // 16) * 2 + core, lax.rem(t, 16))

    def greet(i, carry):
        pl.semaphore_signal(barrier, inc=1, device_id=peer(i), device_id_type=MESH)
        return carry

    lax.fori_loop(1, CHIPS, greet, 0)
    for other in (north, south):
        pl.semaphore_signal(barrier, inc=1, device_id=(other, lon), device_id_type=MESH)
    pl.semaphore_wait(barrier, CHIPS + 1)

    def block_copy(i):
        return pltpu.make_async_remote_copy(
            src_ref=send.at[i], dst_ref=recv.at[i], send_sem=send_sem,
            recv_sem=recv_sem.at[i // GROUP], device_id=peer(i), device_id_type=MESH,
        )

    def post(i, carry):
        block_copy(i).start()
        return carry

    lax.fori_loop(1, CHIPS, post, 0)
    own = pltpu.make_async_copy(send.at[0], recv.at[0], self_sem)
    own.start()

    high = conv[...].astype(BF16).astype(F32)
    mixer[...] = jnp.zeros((256, LANES), F32)
    mixer[0:LEV, 0:LEV] = high
    mixer[LEV : 2 * LEV, 0:LEV] = high
    mixer[2 * LEV : 3 * LEV, 0:LEV] = conv[...] - high
    mix = jnp.transpose(mixer[...])[0:LEV].astype(BF16)
    lev2 = iota((LEV, 2 * LANES), 0)
    lane = iota((LEV, LANES), 1)

    def physics(x, f, d):
        x1 = x.astype(BF16).astype(F32)
        stack = jnp.concatenate([x1, x - x1, x1, jnp.zeros((40, 2 * LANES), F32)], axis=0)
        z = jnp.dot(mix, stack.astype(BF16), preferred_element_type=F32)
        m = x + f * z
        above = jnp.where(lev2 == LEV - 1, m, pltpu.roll(m, LEV - 1, 0))
        below = jnp.where(lev2 == 0, m, pltpu.roll(m, 1, 0))
        return m + d * (above - 2.0 * m + below)

    def column_step(e, load):
        def pair(j, packed):
            r0 = 2 * j
            f = jnp.concatenate([flx[pl.ds(r0, 1), :], flx[pl.ds(r0 + 1, 1), :]], axis=1)
            d = jnp.concatenate([dif[pl.ds(r0, 1), :], dif[pl.ds(r0 + 1, 1), :]], axis=1)
            for t in range(TR):
                x = jnp.concatenate([load(t, r0), load(t, r0 + 1)], axis=1)
                y = physics(x, f, d)
                for k in range(2):
                    part = y[:, k * LANES : (k + 1) * LANES]
                    field[e, r0 + k + 1, t * LEV : (t + 1) * LEV, :] = part
                    at = 2 * (t * CLAT + r0 + k)
                    turned = pltpu.roll(part, at + 1, 1)
                    packed = jnp.where((lane == at) | (lane == at + 1), turned, packed)
            return packed

        return lax.fori_loop(0, CLAT // 2, pair, jnp.zeros((LEV, LANES), F32))

    def halo_copies(e):
        def rc(src, dst, k, dev):
            return pltpu.make_async_remote_copy(
                src_ref=src, dst_ref=dst, send_sem=halo_send.at[e, k],
                recv_sem=halo_recv.at[e, k], device_id=dev, device_id_type=MESH,
            )

        return [
            rc(edges.at[e], west_in.at[e], 0, (lat, east)),
            rc(edges.at[e], east_in.at[e], 1, (lat, west)),
            rc(field.at[e, CLAT], field.at[e, 0], 2, (north, lon)),
            rc(field.at[e, 1], field.at[e, CLAT + 1], 3, (south, lon)),
        ] + ([rc(cn_edge, cn_south, 4, (north, lon))] if e == 0 else [])

    def merged(e):
        return jnp.where(
            jnp.bitwise_and(lane, 1) == 0, west_in[e], pltpu.roll(east_in[e], LANES - 2, 1)
        )

    def advected(e, r, t, halo, g):
        at = 2 * (t * CLAT + r)
        turned = pltpu.roll(halo, lax.rem(2 * LANES - at, LANES), 1)
        rows = pl.ds(t * LEV, LEV)
        c = field[e, r + 1, rows, :]
        n = field[e, r + 2, rows, :]
        s = field[e, r, rows, :]
        ea = jnp.where(lane == LANES - 1, turned, pltpu.roll(c, LANES - 1, 1))
        we = jnp.where(lane == 0, turned, pltpu.roll(c, 1, 1))
        return c + g[0] * (ea - c) + g[1] * (c - we) + g[2] * (n - c) + g[3] * (c - s)

    packed = column_step(0, lambda t, r: adj[pl.ds(t * LEV * CLAT + r, LEV, stride=CLAT), :])

    def face_edge(r, packed):
        at = 64 + 2 * r
        turned = pltpu.roll(ce[pl.ds(r, LEV, stride=CLAT), :], at + 1, 1)
        return jnp.where(lane == at, turned, packed)

    edges[0] = lax.fori_loop(0, CLAT, face_edge, packed)
    cn_edge[...] = cn[pl.ds(CLAT - 1, LEV, stride=CLAT), :]
    first_halo = halo_copies(0)
    for copy in first_halo:
        copy.start()
    for copy in first_halo:
        copy.wait()
    halo0 = merged(0)

    def first_row(r, carry):
        e_face = ce[pl.ds(r, LEV, stride=CLAT), :]
        turned = pltpu.roll(halo0, lax.rem(2 * LANES - 64 - 2 * r, LANES), 1)
        w_face = jnp.where(lane == 0, turned, pltpu.roll(e_face, 1, 1))
        n_face = cn[pl.ds(r, LEV, stride=CLAT), :]
        top = jnp.logical_and(lat == 7, r == CLAT - 1)
        n_face = jnp.where(top, 0.0, n_face)
        s_face = jnp.where(r == 0, cn_south[...], cn[pl.ds(jnp.maximum(r - 1, 0), LEV, stride=CLAT), :])
        s_face = jnp.where(jnp.logical_and(lat == 0, r == 0), 0.0, s_face)
        g = (
            jnp.maximum(e_face, 0.0), jnp.minimum(w_face, 0.0),
            jnp.maximum(n_face, 0.0), jnp.minimum(s_face, 0.0),
        )
        for k in range(4):
            gains[k, r] = g[k]
        for t in range(TR):
            acc[r, t * LEV : (t + 1) * LEV, :] = advected(0, r, t, halo0, g)
        return carry

    lax.fori_loop(0, CLAT, first_row, 0)

    row_id = iota((LANES, LANES), 0)
    eye = (row_id == iota((LANES, LANES), 1)).astype(F32).astype(BF16)
    cell = iota((LANES, ROWS), 0).astype(F32)
    clane = iota((16, LANES), 1)

    def place_group(blocks, tiles):
        parts = []
        for h in range(GROUP // 8):
            s = [tiles[h * 8 + k].astype(F32) for k in range(8)]
            parts.append(jnp.where(clane < 48, s[0], jnp.where(clane < 96, s[1], s[2])))
            parts.append(
                jnp.where(clane < 16, s[2], jnp.where(clane < 64, s[3], jnp.where(clane < 112, s[4], s[5])))
            )
            parts.append(jnp.where(clane < 32, s[5], jnp.where(clane < 80, s[6], s[7])))
        codes[...] = jnp.concatenate(parts, axis=1)
        shift = codes[pl.ds(core * 3, 1), :].astype(jnp.int32)
        lat_row = codes[pl.ds(core * 3 + 1, 1), :]
        lon_col = codes[pl.ds(core * 3 + 2, 1), :]
        turned = lax.dot_general(eye, blocks, (((1,), (1,)), ((), ())), preferred_element_type=F32)
        placed = []
        for t in range(TR):
            x = jnp.concatenate([turned[t * SPAN : (t + 1) * SPAN], jnp.zeros((8, ROWS), F32)], axis=0)
            for bit in (1, 2, 4):
                x = jnp.where(jnp.bitwise_and(shift, bit) != 0, pltpu.roll(x, bit, 0), x)
            x8 = jnp.concatenate([jnp.zeros((8, ROWS), F32), x[: LEV - 8]], axis=0)
            placed.append(jnp.where(jnp.bitwise_and(shift, 8) != 0, x8, x))
        placed = jnp.concatenate(placed, axis=0).astype(BF16)
        hot = jnp.where(cell == lon_col, 1.0, 0.0).astype(BF16)

        def rows_pair(j, carry):
            two = []
            for k in range(2):
                mine = jnp.where(lat_row == (2 * j + k).astype(F32), 1.0, 0.0).astype(BF16)
                two.append(hot * mine)
            res = lax.dot_general(
                placed, jnp.concatenate(two, axis=0), (((1,), (1,)), ((), ())),
                preferred_element_type=F32,
            )
            acc[2 * j] += res[:, :LANES]
            acc[2 * j + 1] += res[:, LANES:]
            return carry

        lax.fori_loop(0, CLAT // 2, rows_pair, 0)

    mine_at = pl.ds(pl.multiple_of(core * CAP, 16), CAP)
    other_at = pl.ds(pl.multiple_of(CAP - core * CAP, 16), CAP)

    def forwards(g):
        at = pl.ds(g * GROUP, GROUP)
        return [
            pltpu.make_async_remote_copy(
                src_ref=recv.at[at, other_at, :], dst_ref=fwd.at[at],
                send_sem=fwd_send.at[0, g], recv_sem=fwd_recv.at[0, g],
                device_id=(sibling, lon), device_id_type=MESH,
            ),
            pltpu.make_async_remote_copy(
                src_ref=recv.at[at, 2 * CAP : BLOCK, :], dst_ref=fwdc.at[at],
                send_sem=fwd_send.at[1, g], recv_sem=fwd_recv.at[1, g],
                device_id=(sibling, lon), device_id_type=MESH,
            ),
        ]

    def arrived(g, lo):
        at = pl.ds(g * GROUP + lo, GROUP - lo)
        pltpu.make_async_remote_copy(
            src_ref=send.at[at], dst_ref=recv.at[at], send_sem=send_sem,
            recv_sem=recv_sem.at[g], device_id=(sibling, lon), device_id_type=MESH,
        ).wait_recv()

    own.wait()
    for g in range(GROUPS):
        arrived(g, 1 if g == 0 else 0)
        for copy in forwards(g):
            copy.start()
        at = pl.ds(g * GROUP, GROUP)
        place_group(recv[at, mine_at, :].reshape(ROWS, LANES), recv[at, 2 * CAP : BLOCK, :])
    for g in range(GROUPS):
        for copy in forwards(g):
            copy.wait_recv()
        at = pl.ds(g * GROUP, GROUP)
        place_group(fwd[at].reshape(ROWS, LANES), fwdc[at])

    edges[1] = column_step(1, lambda t, r: acc[r, t * LEV : (t + 1) * LEV, :])
    second_halo = halo_copies(1)
    for copy in second_halo:
        copy.start()
    for copy in second_halo:
        copy.wait()
    halo1 = merged(1)

    def second_row(r, carry):
        g = tuple(gains[k, r] for k in range(4))
        for t in range(TR):
            y = advected(1, r, t, halo1, g)
            out[pl.ds(t * LEV * CLAT + r, LEV, stride=CLAT), :] = y
            flux[pl.ds(t * CLAT + r, 1), :] = y[0:1] + acc[r, t * LEV : t * LEV + 1, :]
        return carry

    lax.fori_loop(0, CLAT, second_row, 0)
    for g in range(GROUPS):
        for copy in forwards(g):
            copy.wait_send()
    every = pl.ds(1, CHIPS - 1)
    pltpu.make_async_remote_copy(
        src_ref=send.at[every], dst_ref=recv.at[every], send_sem=send_sem,
        recv_sem=recv_sem.at[0], device_id=(sibling, lon), device_id_type=MESH,
    ).wait_send()


def local(adjoint_state, courant_east, courant_north, diffusion, convective_flux, convection,
          sounding_forcing, sounding_column, sounding_level, owner_counts):
    send = pack(owner_counts, sounding_forcing, sounding_column, sounding_level)
    vmem = pl.BlockSpec(memory_space=pltpu.VMEM)
    dma = pltpu.SemaphoreType.DMA
    out, flux = pl.pallas_call(
        main_kernel,
        out_shape=(
            jax.ShapeDtypeStruct((TR * LEV * CLAT, LANES), F32),
            jax.ShapeDtypeStruct((TR * CLAT, LANES), F32),
        ),
        in_specs=[vmem] * 7,
        out_specs=(vmem, vmem),
        scratch_shapes=[
            pltpu.VMEM((CHIPS, BLOCK, LANES), BF16),
            pltpu.VMEM((CHIPS, CAP, LANES), BF16),
            pltpu.VMEM((CHIPS, 16, LANES), BF16),
            pltpu.VMEM((CLAT, TR * LEV, LANES), F32),
            pltpu.VMEM((2, CLAT + 2, TR * LEV, LANES), F32),
            pltpu.VMEM((4, CLAT, LEV, LANES), F32),
            pltpu.VMEM((256, LANES), F32),
            pltpu.VMEM((16, ROWS), F32),
            pltpu.VMEM((2, LEV, LANES), F32),
            pltpu.VMEM((2, LEV, LANES), F32),
            pltpu.VMEM((2, LEV, LANES), F32),
            pltpu.VMEM((LEV, LANES), F32),
            pltpu.VMEM((LEV, LANES), F32),
            dma,
            dma((GROUPS,)),
            dma((2, GROUPS)),
            dma((2, GROUPS)),
            dma((2, 5)),
            dma((2, 5)),
            dma,
        ],
        compiler_params=pltpu.CompilerParams(
            collective_id=0, has_side_effects=True, vmem_limit_bytes=48 << 20
        ),
        name="transport",
    )(
        adjoint_state.reshape(TR * LEV * CLAT, LANES),
        courant_east.reshape(LEV * CLAT, LANES),
        courant_north.reshape(LEV * CLAT, LANES),
        diffusion, convective_flux, convection, send,
    )
    return out.reshape(TR, LEV, CLAT, LANES), flux.reshape(TR, CLAT, LANES)


def solution(mesh):
    return jax.shard_map(
        local,
        mesh=mesh,
        in_specs=(
            P(None, None, "lat", "lon"),
            P(None, "lat", "lon"),
            P(None, "lat", "lon"),
            P("lat", "lon"),
            P("lat", "lon"),
            P(),
            P(("lat", "lon"), None),
            P(("lat", "lon")),
            P(("lat", "lon")),
            P(("lat", "lon"), None),
        ),
        out_specs=(P(None, None, "lat", "lon"), P(None, "lat", "lon")),
        check_vma=False,
    )
```

```python
import jax
import jax.numpy as jnp
from jax import lax
from jax.experimental import pallas as pl
from jax.experimental.pallas import tpu as pltpu
from jax.sharding import PartitionSpec as P

TR = 2
LEV = 72
SPAN = 64
CAP = 48
CLAT = 16
LANES = 128
CHIPS = 64
STRIDE = 45
BLOCK = 2 * CAP + 16
GROUP = 16
GROUPS = CHIPS // GROUP
ROWS = GROUP * CAP
F32 = jnp.float32
BF16 = jnp.bfloat16
MESH = pl.DeviceIdType.MESH


def place():
    lat = lax.axis_index("lat")
    lon = lax.axis_index("lon")
    return lat, lon, lax.rem(lat, 2), (lat // 2) * 16 + lon


def peer_chip(chip, step):
    return jnp.bitwise_xor(chip, lax.rem(step * STRIDE, CHIPS))


def iota(shape, axis):
    return lax.broadcasted_iota(jnp.int32, shape, axis)


def main_kernel(
    counts, adj_hbm, ce_hbm, cn_hbm, dif_hbm, flx_hbm, conv_hbm, forcing_hbm, column_hbm, level_hbm,
    out, flux,
    adj, ce, cn, dif, flx, conv, forcing, column, level,
    rows_f32, targets, starts, load_sem,
    send, recv, fwd, fwdc, acc, field, gains, mixer, codes, edges, west_in, east_in, cn_edge, cn_south,
    send_sem, recv_sem, fwd_send, fwd_recv, halo_send, halo_recv, self_sem,
):
    lat, lon, core, chip = place()
    north = lax.rem(lat + 1, 8)
    south = lax.rem(lat + 7, 8)
    east = lax.rem(lon + 1, 16)
    west = lax.rem(lon + 15, 16)
    sibling = lat + 1 - 2 * core
    loads = [
        pltpu.make_async_copy(src, dst, load_sem.at[k])
        for k, (src, dst) in enumerate((
            (forcing_hbm, forcing), (column_hbm, column), (level_hbm, level), (adj_hbm, adj), (conv_hbm, conv),
            (dif_hbm, dif), (flx_hbm, flx), (ce_hbm, ce), (cn_hbm, cn),
        ))
    ]
    for copy in loads:
        copy.start()
    barrier = pltpu.get_barrier_semaphore()

    def peer(i):
        t = peer_chip(chip, i)
        return ((t // 16) * 2 + core, lax.rem(t, 16))

    def greet(i, carry):
        pl.semaphore_signal(barrier, inc=1, device_id=peer(i), device_id_type=MESH)
        return carry

    lax.fori_loop(1, CHIPS, greet, 0)
    for other in (north, south):
        pl.semaphore_signal(barrier, inc=1, device_id=(other, lon), device_id_type=MESH)

    def prefix(o, total):
        starts[o] = total
        return total + counts[0, o]

    lax.fori_loop(0, 128, prefix, jnp.int32(0))
    for copy in loads[:3]:
        copy.wait()

    def widen(i, carry):
        at = pl.ds(pl.multiple_of(i * 256, 256), 256)
        rows_f32[at, :] = forcing[at, :].astype(F32)
        return carry

    lax.fori_loop(0, forcing.shape[0] // 256, widen, 0)
    targets[0:48, :] = level[...] * 2048 + column[...]
    targets[48:56, :] = jnp.zeros((8, LANES), jnp.int32)
    lane8 = iota((8, LANES), 1)
    sub16 = iota((16, LANES), 0)

    def pack(i):
        t = peer_chip(chip, i)
        first_lane = lax.rem(i * CAP, LANES)
        slot = jnp.bitwise_and(lane8 - first_lane, LANES - 1)
        tile = jnp.zeros((16, LANES), F32)
        for dc in range(2):
            owner = ((t // 16) * 2 + dc) * 16 + lax.rem(t, 16)
            start = starts[owner]
            count = counts[0, owner]
            send[i, dc * CAP : (dc + 1) * CAP, :] = rows_f32[pl.ds(start, CAP), :].astype(BF16)
            row = start // LANES
            off = lax.rem(start, LANES)
            turn = lax.rem(first_lane - off + LANES, LANES)
            near = pltpu.roll(jnp.broadcast_to(targets[pl.ds(row, 1), :], (8, LANES)), turn, 1)
            far = pltpu.roll(jnp.broadcast_to(targets[pl.ds(row + 1, 1), :], (8, LANES)), turn, 1)
            code = jnp.where(slot < LANES - off, near, far)
            valid = slot < count
            shift = jnp.where(valid, jnp.right_shift(code, 11), 0)
            lat_row = jnp.where(valid, jnp.bitwise_and(jnp.right_shift(code, 7), 15), -1)
            lon_col = jnp.bitwise_and(code, 127)
            for k, part in enumerate((shift, lat_row, lon_col)):
                part = part.astype(F32)
                both = jnp.concatenate([part, part], axis=0)
                tile = jnp.where(sub16 == dc * 3 + k, both, tile)
        send[i, 2 * CAP : BLOCK, :] = tile.astype(BF16)

    def block_copy(i):
        return pltpu.make_async_remote_copy(
            src_ref=send.at[i], dst_ref=recv.at[i], send_sem=send_sem,
            recv_sem=recv_sem.at[i // GROUP], device_id=peer(i), device_id_type=MESH,
        )

    pack(0)
    own = pltpu.make_async_copy(send.at[0], recv.at[0], self_sem)
    own.start()
    pl.semaphore_wait(barrier, CHIPS + 1)

    def post(i, carry):
        pack(i)
        block_copy(i).start()
        return carry

    lax.fori_loop(1, CHIPS, post, 0)
    for copy in loads[3:]:
        copy.wait()

    high = conv[...].astype(BF16).astype(F32)
    mixer[...] = jnp.zeros((256, LANES), F32)
    mixer[0:LEV, 0:LEV] = high
    mixer[LEV : 2 * LEV, 0:LEV] = high
    mixer[2 * LEV : 3 * LEV, 0:LEV] = conv[...] - high
    mix = jnp.transpose(mixer[...])[0:LEV].astype(BF16)
    lev2 = iota((LEV, 2 * LANES), 0)
    lane = iota((LEV, LANES), 1)

    def physics(x, f, d):
        x1 = x.astype(BF16).astype(F32)
        stack = jnp.concatenate([x1, x - x1, x1, jnp.zeros((40, 2 * LANES), F32)], axis=0)
        z = jnp.dot(mix, stack.astype(BF16), preferred_element_type=F32)
        m = x + f * z
        above = jnp.where(lev2 == LEV - 1, m, pltpu.roll(m, LEV - 1, 0))
        below = jnp.where(lev2 == 0, m, pltpu.roll(m, 1, 0))
        return m + d * (above - 2.0 * m + below)

    def column_step(e, load):
        def pair(j, packed):
            r0 = 2 * j
            f = jnp.concatenate([flx[pl.ds(r0, 1), :], flx[pl.ds(r0 + 1, 1), :]], axis=1)
            d = jnp.concatenate([dif[pl.ds(r0, 1), :], dif[pl.ds(r0 + 1, 1), :]], axis=1)
            for t in range(TR):
                x = jnp.concatenate([load(t, r0), load(t, r0 + 1)], axis=1)
                y = physics(x, f, d)
                for k in range(2):
                    part = y[:, k * LANES : (k + 1) * LANES]
                    field[e, r0 + k + 1, t * LEV : (t + 1) * LEV, :] = part
                    at = 2 * (t * CLAT + r0 + k)
                    turned = pltpu.roll(part, at + 1, 1)
                    packed = jnp.where((lane == at) | (lane == at + 1), turned, packed)
            return packed

        return lax.fori_loop(0, CLAT // 2, pair, jnp.zeros((LEV, LANES), F32))

    def halo_copies(e):
        def rc(src, dst, k, dev):
            return pltpu.make_async_remote_copy(
                src_ref=src, dst_ref=dst, send_sem=halo_send.at[e, k],
                recv_sem=halo_recv.at[e, k], device_id=dev, device_id_type=MESH,
            )

        return [
            rc(edges.at[e], west_in.at[e], 0, (lat, east)),
            rc(edges.at[e], east_in.at[e], 1, (lat, west)),
            rc(field.at[e, CLAT], field.at[e, 0], 2, (north, lon)),
            rc(field.at[e, 1], field.at[e, CLAT + 1], 3, (south, lon)),
        ] + ([rc(cn_edge, cn_south, 4, (north, lon))] if e == 0 else [])

    def merged(e):
        return jnp.where(
            jnp.bitwise_and(lane, 1) == 0, west_in[e], pltpu.roll(east_in[e], LANES - 2, 1)
        )

    def advected(e, r, t, halo, g):
        at = 2 * (t * CLAT + r)
        turned = pltpu.roll(halo, lax.rem(2 * LANES - at, LANES), 1)
        rows = pl.ds(t * LEV, LEV)
        c = field[e, r + 1, rows, :]
        n = field[e, r + 2, rows, :]
        s = field[e, r, rows, :]
        ea = jnp.where(lane == LANES - 1, turned, pltpu.roll(c, LANES - 1, 1))
        we = jnp.where(lane == 0, turned, pltpu.roll(c, 1, 1))
        return c + g[0] * (ea - c) + g[1] * (c - we) + g[2] * (n - c) + g[3] * (c - s)

    packed = column_step(0, lambda t, r: adj[pl.ds(t * LEV * CLAT + r, LEV, stride=CLAT), :])

    def face_edge(r, packed):
        at = 64 + 2 * r
        turned = pltpu.roll(ce[pl.ds(r, LEV, stride=CLAT), :], at + 1, 1)
        return jnp.where(lane == at, turned, packed)

    edges[0] = lax.fori_loop(0, CLAT, face_edge, packed)
    cn_edge[...] = cn[pl.ds(CLAT - 1, LEV, stride=CLAT), :]
    first_halo = halo_copies(0)
    for copy in first_halo:
        copy.start()
    for copy in first_halo:
        copy.wait()
    halo0 = merged(0)

    def first_row(r, carry):
        e_face = ce[pl.ds(r, LEV, stride=CLAT), :]
        turned = pltpu.roll(halo0, lax.rem(2 * LANES - 64 - 2 * r, LANES), 1)
        w_face = jnp.where(lane == 0, turned, pltpu.roll(e_face, 1, 1))
        n_face = cn[pl.ds(r, LEV, stride=CLAT), :]
        top = jnp.logical_and(lat == 7, r == CLAT - 1)
        n_face = jnp.where(top, 0.0, n_face)
        s_face = jnp.where(r == 0, cn_south[...], cn[pl.ds(jnp.maximum(r - 1, 0), LEV, stride=CLAT), :])
        s_face = jnp.where(jnp.logical_and(lat == 0, r == 0), 0.0, s_face)
        g = (
            jnp.maximum(e_face, 0.0), jnp.minimum(w_face, 0.0),
            jnp.maximum(n_face, 0.0), jnp.minimum(s_face, 0.0),
        )
        for k in range(4):
            gains[k, r] = g[k]
        for t in range(TR):
            acc[r, t * LEV : (t + 1) * LEV, :] = advected(0, r, t, halo0, g)
        return carry

    lax.fori_loop(0, CLAT, first_row, 0)

    row_id = iota((LANES, LANES), 0)
    eye = (row_id == iota((LANES, LANES), 1)).astype(F32).astype(BF16)
    cells = iota((ROWS, 2 * LANES), 1).astype(F32)
    clane = iota((16, LANES), 1)

    def place_group(blocks, tiles):
        parts = []
        for h in range(GROUP // 8):
            s = [tiles[h * 8 + k].astype(F32) for k in range(8)]
            parts.append(jnp.where(clane < 48, s[0], jnp.where(clane < 96, s[1], s[2])))
            parts.append(
                jnp.where(clane < 16, s[2], jnp.where(clane < 64, s[3], jnp.where(clane < 112, s[4], s[5])))
            )
            parts.append(jnp.where(clane < 32, s[5], jnp.where(clane < 80, s[6], s[7])))
        codes[...] = jnp.concatenate(parts, axis=1)
        shift = codes[pl.ds(core * 3, 1), :].astype(jnp.int32)
        lat_row = codes[pl.ds(core * 3 + 1, 1), :]
        lon_col = codes[pl.ds(core * 3 + 2, 1), :]
        turned = lax.dot_general(eye, blocks, (((1,), (1,)), ((), ())), preferred_element_type=F32)
        placed = []
        for t in range(TR):
            x = jnp.concatenate([turned[t * SPAN : (t + 1) * SPAN], jnp.zeros((8, ROWS), F32)], axis=0)
            for bit in (1, 2, 4):
                x = jnp.where(jnp.bitwise_and(shift, bit) != 0, pltpu.roll(x, bit, 0), x)
            x8 = jnp.concatenate([jnp.zeros((8, ROWS), F32), x[: LEV - 8]], axis=0)
            placed.append(jnp.where(jnp.bitwise_and(shift, 8) != 0, x8, x))
        placed = jnp.concatenate(placed, axis=0).astype(BF16)
        parity = jnp.bitwise_and(lat_row.astype(jnp.int32), 1).astype(F32)
        cell = jnp.broadcast_to(parity * LANES + lon_col, (8, ROWS))
        hot = jnp.where(jnp.transpose(cell)[:, 0:1] == cells, 1.0, 0.0).astype(BF16)
        for j in range(CLAT // 2):
            mine = jnp.where((lat_row == 2 * j) | (lat_row == 2 * j + 1), 1.0, 0.0).astype(BF16)
            res = jnp.dot(placed * mine, hot, preferred_element_type=F32)
            acc[2 * j] += res[:, :LANES]
            acc[2 * j + 1] += res[:, LANES:]

    mine_at = pl.ds(pl.multiple_of(core * CAP, 16), CAP)
    other_at = pl.ds(pl.multiple_of(CAP - core * CAP, 16), CAP)

    def forwards(g):
        at = pl.ds(g * GROUP, GROUP)
        return [
            pltpu.make_async_remote_copy(
                src_ref=recv.at[at, other_at, :], dst_ref=fwd.at[at],
                send_sem=fwd_send.at[0, g], recv_sem=fwd_recv.at[0, g],
                device_id=(sibling, lon), device_id_type=MESH,
            ),
            pltpu.make_async_remote_copy(
                src_ref=recv.at[at, 2 * CAP : BLOCK, :], dst_ref=fwdc.at[at],
                send_sem=fwd_send.at[1, g], recv_sem=fwd_recv.at[1, g],
                device_id=(sibling, lon), device_id_type=MESH,
            ),
        ]

    def arrived(g, lo):
        at = pl.ds(g * GROUP + lo, GROUP - lo)
        pltpu.make_async_remote_copy(
            src_ref=send.at[at], dst_ref=recv.at[at], send_sem=send_sem,
            recv_sem=recv_sem.at[g], device_id=(sibling, lon), device_id_type=MESH,
        ).wait_recv()

    own.wait()
    for g in range(GROUPS):
        arrived(g, 1 if g == 0 else 0)
        for copy in forwards(g):
            copy.start()
        at = pl.ds(g * GROUP, GROUP)
        place_group(recv[at, mine_at, :].reshape(ROWS, LANES), recv[at, 2 * CAP : BLOCK, :])
    for g in range(GROUPS):
        for copy in forwards(g):
            copy.wait_recv()
        at = pl.ds(g * GROUP, GROUP)
        place_group(fwd[at].reshape(ROWS, LANES), fwdc[at])

    edges[1] = column_step(1, lambda t, r: acc[r, t * LEV : (t + 1) * LEV, :])
    second_halo = halo_copies(1)
    for copy in second_halo:
        copy.start()
    for copy in second_halo:
        copy.wait()
    halo1 = merged(1)

    def second_row(r, carry):
        g = tuple(gains[k, r] for k in range(4))
        for t in range(TR):
            y = advected(1, r, t, halo1, g)
            out[pl.ds(t * LEV * CLAT + r, LEV, stride=CLAT), :] = y
            flux[pl.ds(t * CLAT + r, 1), :] = y[0:1] + acc[r, t * LEV : t * LEV + 1, :]
        return carry

    lax.fori_loop(0, CLAT, second_row, 0)
    for g in range(GROUPS):
        for copy in forwards(g):
            copy.wait_send()
    every = pl.ds(1, CHIPS - 1)
    pltpu.make_async_remote_copy(
        src_ref=send.at[every], dst_ref=recv.at[every], send_sem=send_sem,
        recv_sem=recv_sem.at[0], device_id=(sibling, lon), device_id_type=MESH,
    ).wait_send()


def local(adjoint_state, courant_east, courant_north, diffusion, convective_flux, convection,
          sounding_forcing, sounding_column, sounding_level, owner_counts):
    vmem = pl.BlockSpec(memory_space=pltpu.VMEM)
    dma = pltpu.SemaphoreType.DMA
    listed = sounding_forcing.shape[0]
    out, flux = pl.pallas_call(
        main_kernel,
        out_shape=(
            jax.ShapeDtypeStruct((TR * LEV * CLAT, LANES), F32),
            jax.ShapeDtypeStruct((TR * CLAT, LANES), F32),
        ),
        in_specs=[pl.BlockSpec(memory_space=pltpu.SMEM)] + [pl.BlockSpec(memory_space=pl.ANY)] * 9,
        out_specs=(vmem, vmem),
        scratch_shapes=[
            pltpu.VMEM((TR * LEV * CLAT, LANES), F32),
            pltpu.VMEM((LEV * CLAT, LANES), F32),
            pltpu.VMEM((LEV * CLAT, LANES), F32),
            pltpu.VMEM((CLAT, LANES), F32),
            pltpu.VMEM((CLAT, LANES), F32),
            pltpu.VMEM((LEV, LEV), F32),
            pltpu.VMEM((listed, LANES), BF16),
            pltpu.VMEM((listed // LANES, LANES), jnp.int32),
            pltpu.VMEM((listed // LANES, LANES), jnp.int32),
            pltpu.VMEM((listed, LANES), F32),
            pltpu.VMEM((56, LANES), jnp.int32),
            pltpu.SMEM((128,), jnp.int32),
            dma((9,)),
            pltpu.VMEM((CHIPS, BLOCK, LANES), BF16),
            pltpu.VMEM((CHIPS, BLOCK, LANES), BF16),
            pltpu.VMEM((CHIPS, CAP, LANES), BF16),
            pltpu.VMEM((CHIPS, 16, LANES), BF16),
            pltpu.VMEM((CLAT, TR * LEV, LANES), F32),
            pltpu.VMEM((2, CLAT + 2, TR * LEV, LANES), F32),
            pltpu.VMEM((4, CLAT, LEV, LANES), F32),
            pltpu.VMEM((256, LANES), F32),
            pltpu.VMEM((16, ROWS), F32),
            pltpu.VMEM((2, LEV, LANES), F32),
            pltpu.VMEM((2, LEV, LANES), F32),
            pltpu.VMEM((2, LEV, LANES), F32),
            pltpu.VMEM((LEV, LANES), F32),
            pltpu.VMEM((LEV, LANES), F32),
            dma,
            dma((GROUPS,)),
            dma((2, GROUPS)),
            dma((2, GROUPS)),
            dma((2, 5)),
            dma((2, 5)),
            dma,
        ],
        compiler_params=pltpu.CompilerParams(
            collective_id=0, has_side_effects=True, vmem_limit_bytes=60 << 20
        ),
        name="transport",
    )(
        owner_counts,
        adjoint_state.reshape(TR * LEV * CLAT, LANES),
        courant_east.reshape(LEV * CLAT, LANES),
        courant_north.reshape(LEV * CLAT, LANES),
        diffusion, convective_flux, convection,
        sounding_forcing,
        sounding_column.reshape(listed // LANES, LANES),
        sounding_level.reshape(listed // LANES, LANES),
    )
    return out.reshape(TR, LEV, CLAT, LANES), flux.reshape(TR, CLAT, LANES)


def solution(mesh):
    return jax.shard_map(
        local,
        mesh=mesh,
        in_specs=(
            P(None, None, "lat", "lon"),
            P(None, "lat", "lon"),
            P(None, "lat", "lon"),
            P("lat", "lon"),
            P("lat", "lon"),
            P(),
            P(("lat", "lon"), None),
            P(("lat", "lon")),
            P(("lat", "lon")),
            P(("lat", "lon"), None),
        ),
        out_specs=(P(None, None, "lat", "lon"), P(None, "lat", "lon")),
        check_vma=False,
    )
```

```python
import jax
import jax.numpy as jnp
from jax import lax
from jax.experimental import pallas as pl
from jax.experimental.pallas import tpu as pltpu
from jax.sharding import PartitionSpec as P

TR = 2
LEV = 72
SPAN = 64
CAP = 48
CLAT = 16
LANES = 128
CHIPS = 64
STRIDE = 45
BLOCK = 2 * CAP + 16
GROUP = 16
GROUPS = CHIPS // GROUP
ROWS = GROUP * CAP
F32 = jnp.float32
BF16 = jnp.bfloat16
MESH = pl.DeviceIdType.MESH


def place():
    lat = lax.axis_index("lat")
    lon = lax.axis_index("lon")
    return lat, lon, jnp.bitwise_and(lat, 1), jnp.right_shift(lat, 1) * 16 + lon


def peer_chip(chip, step):
    return jnp.bitwise_xor(chip, jnp.bitwise_and(step * STRIDE, CHIPS - 1))


def iota(shape, axis):
    return lax.broadcasted_iota(jnp.int32, shape, axis)


def main_kernel(
    counts, adj_hbm, ce_hbm, cn_hbm, dif_hbm, flx_hbm, conv_hbm, forcing_hbm, column_hbm, level_hbm,
    out, flux,
    adj, ce, cn, dif, flx, conv, forcing, column, level,
    rows_f32, targets, starts, load_sem,
    send, recv, fwd, fwdc, acc, field, gains, mixer, codes, edges, west_in, east_in, cn_edge, cn_south,
    send_sem, recv_sem, fwd_send, fwd_recv, halo_send, halo_recv, self_sem,
):
    lat, lon, core, chip = place()
    north = lax.rem(lat + 1, 8)
    south = lax.rem(lat + 7, 8)
    east = lax.rem(lon + 1, 16)
    west = lax.rem(lon + 15, 16)
    sibling = lat + 1 - 2 * core
    loads = [
        pltpu.make_async_copy(src, dst, load_sem.at[k])
        for k, (src, dst) in enumerate((
            (forcing_hbm, forcing), (column_hbm, column), (level_hbm, level), (adj_hbm, adj), (conv_hbm, conv),
            (dif_hbm, dif), (flx_hbm, flx), (ce_hbm, ce), (cn_hbm, cn),
        ))
    ]
    for copy in loads:
        copy.start()
    barrier = pltpu.get_barrier_semaphore()

    def peer(i):
        t = peer_chip(chip, i)
        return (jnp.right_shift(t, 4) * 2 + core, jnp.bitwise_and(t, 15))

    def greet(i, carry):
        pl.semaphore_signal(barrier, inc=1, device_id=peer(i), device_id_type=MESH)
        return carry

    lax.fori_loop(1, CHIPS, greet, 0, unroll=1)
    for other in (north, south):
        pl.semaphore_signal(barrier, inc=1, device_id=(other, lon), device_id_type=MESH)

    def prefix(o, total):
        starts[o] = total
        return total + counts[0, o]

    lax.fori_loop(0, 128, prefix, jnp.int32(0), unroll=8)
    for copy in loads[:3]:
        copy.wait()

    def widen(i, carry):
        at = pl.ds(pl.multiple_of(i * 256, 256), 256)
        rows_f32[at, :] = forcing[at, :].astype(F32)
        return carry

    lax.fori_loop(0, forcing.shape[0] // 256, widen, 0, unroll=2)
    targets[0:48, :] = level[...] * 2048 + column[...]
    targets[48:56, :] = jnp.zeros((8, LANES), jnp.int32)
    lane8 = iota((8, LANES), 1)
    sub16 = iota((16, LANES), 0)

    def pack(i):
        t = peer_chip(chip, i)
        first_lane = jnp.bitwise_and(i * CAP, LANES - 1)
        slot = jnp.bitwise_and(lane8 - first_lane, LANES - 1)
        tile = jnp.zeros((16, LANES), F32)
        for dc in range(2):
            owner = (jnp.right_shift(t, 4) * 2 + dc) * 16 + jnp.bitwise_and(t, 15)
            start = starts[owner]
            count = counts[0, owner]
            send[i, dc * CAP : (dc + 1) * CAP, :] = rows_f32[pl.ds(start, CAP), :].astype(BF16)
            row = jnp.right_shift(start, 7)
            off = jnp.bitwise_and(start, LANES - 1)
            turn = jnp.bitwise_and(first_lane - off + LANES, LANES - 1)
            near = pltpu.roll(jnp.broadcast_to(targets[pl.ds(row, 1), :], (8, LANES)), turn, 1)
            far = pltpu.roll(jnp.broadcast_to(targets[pl.ds(row + 1, 1), :], (8, LANES)), turn, 1)
            code = jnp.where(slot < LANES - off, near, far)
            valid = slot < count
            shift = jnp.where(valid, jnp.right_shift(code, 11), 0)
            lat_row = jnp.where(valid, jnp.bitwise_and(jnp.right_shift(code, 7), 15), -1)
            lon_col = jnp.bitwise_and(code, 127)
            for k, part in enumerate((shift, lat_row, lon_col)):
                part = part.astype(F32)
                both = jnp.concatenate([part, part], axis=0)
                tile = jnp.where(sub16 == dc * 3 + k, both, tile)
        send[i, 2 * CAP : BLOCK, :] = tile.astype(BF16)

    def block_copy(i):
        return pltpu.make_async_remote_copy(
            src_ref=send.at[i], dst_ref=recv.at[i], send_sem=send_sem,
            recv_sem=recv_sem.at[jnp.right_shift(i, 4)], device_id=peer(i), device_id_type=MESH,
        )

    pack(0)
    own = pltpu.make_async_copy(send.at[0], recv.at[0], self_sem)
    own.start()
    pl.semaphore_wait(barrier, CHIPS + 1)

    def post(i, carry):
        pack(i)
        block_copy(i).start()
        return carry

    lax.fori_loop(1, CHIPS, post, 0, unroll=1)
    for copy in loads[3:]:
        copy.wait()

    high = conv[...].astype(BF16).astype(F32)
    mixer[...] = jnp.zeros((256, LANES), F32)
    mixer[0:LEV, 0:LEV] = high
    mixer[LEV : 2 * LEV, 0:LEV] = high
    mixer[2 * LEV : 3 * LEV, 0:LEV] = conv[...] - high
    mix = jnp.transpose(mixer[...])[0:LEV].astype(BF16)
    lev2 = iota((LEV, 2 * LANES), 0)
    lane = iota((LEV, LANES), 1)

    def physics(x, f, d):
        x1 = x.astype(BF16).astype(F32)
        stack = jnp.concatenate([x1, x - x1, x1, jnp.zeros((40, 2 * LANES), F32)], axis=0)
        z = jnp.dot(mix, stack.astype(BF16), preferred_element_type=F32)
        m = x + f * z
        above = jnp.where(lev2 == LEV - 1, m, pltpu.roll(m, LEV - 1, 0))
        below = jnp.where(lev2 == 0, m, pltpu.roll(m, 1, 0))
        return m + d * (above - 2.0 * m + below)

    def column_step(e, load):
        def pair(j, packed):
            r0 = 2 * j
            f = jnp.concatenate([flx[pl.ds(r0, 1), :], flx[pl.ds(r0 + 1, 1), :]], axis=1)
            d = jnp.concatenate([dif[pl.ds(r0, 1), :], dif[pl.ds(r0 + 1, 1), :]], axis=1)
            for t in range(TR):
                x = jnp.concatenate([load(t, r0), load(t, r0 + 1)], axis=1)
                y = physics(x, f, d)
                for k in range(2):
                    part = y[:, k * LANES : (k + 1) * LANES]
                    field[e, r0 + k + 1, t * LEV : (t + 1) * LEV, :] = part
                    at = 2 * (t * CLAT + r0 + k)
                    turned = pltpu.roll(part, at + 1, 1)
                    packed = jnp.where((lane == at) | (lane == at + 1), turned, packed)
            return packed

        return lax.fori_loop(0, CLAT // 2, pair, jnp.zeros((LEV, LANES), F32), unroll=8)

    def halo_copies(e):
        def rc(src, dst, k, dev):
            return pltpu.make_async_remote_copy(
                src_ref=src, dst_ref=dst, send_sem=halo_send.at[e, k],
                recv_sem=halo_recv.at[e, k], device_id=dev, device_id_type=MESH,
            )

        return [
            rc(edges.at[e], west_in.at[e], 0, (lat, east)),
            rc(edges.at[e], east_in.at[e], 1, (lat, west)),
            rc(field.at[e, CLAT], field.at[e, 0], 2, (north, lon)),
            rc(field.at[e, 1], field.at[e, CLAT + 1], 3, (south, lon)),
        ] + ([rc(cn_edge, cn_south, 4, (north, lon))] if e == 0 else [])

    def merged(e):
        return jnp.where(
            jnp.bitwise_and(lane, 1) == 0, west_in[e], pltpu.roll(east_in[e], LANES - 2, 1)
        )

    def advected(e, r, t, halo, g):
        at = 2 * (t * CLAT + r)
        turned = pltpu.roll(halo, lax.rem(2 * LANES - at, LANES), 1)
        rows = pl.ds(t * LEV, LEV)
        c = field[e, r + 1, rows, :]
        n = field[e, r + 2, rows, :]
        s = field[e, r, rows, :]
        ea = jnp.where(lane == LANES - 1, turned, pltpu.roll(c, LANES - 1, 1))
        we = jnp.where(lane == 0, turned, pltpu.roll(c, 1, 1))
        return c + g[0] * (ea - c) + g[1] * (c - we) + g[2] * (n - c) + g[3] * (c - s)

    packed = column_step(0, lambda t, r: adj[pl.ds(t * LEV * CLAT + r, LEV, stride=CLAT), :])

    def face_edge(r, packed):
        at = 64 + 2 * r
        turned = pltpu.roll(ce[pl.ds(r, LEV, stride=CLAT), :], at + 1, 1)
        return jnp.where(lane == at, turned, packed)

    edges[0] = lax.fori_loop(0, CLAT, face_edge, packed, unroll=True)
    cn_edge[...] = cn[pl.ds(CLAT - 1, LEV, stride=CLAT), :]
    first_halo = halo_copies(0)
    for copy in first_halo:
        copy.start()

    def first_row(r, halo0):
        e_face = ce[pl.ds(r, LEV, stride=CLAT), :]
        turned = pltpu.roll(halo0, lax.rem(2 * LANES - 64 - 2 * r, LANES), 1)
        w_face = jnp.where(lane == 0, turned, pltpu.roll(e_face, 1, 1))
        n_face = cn[pl.ds(r, LEV, stride=CLAT), :]
        top = jnp.logical_and(lat == 7, r == CLAT - 1)
        n_face = jnp.where(top, 0.0, n_face)
        s_face = jnp.where(r == 0, cn_south[...], cn[pl.ds(jnp.maximum(r - 1, 0), LEV, stride=CLAT), :])
        s_face = jnp.where(jnp.logical_and(lat == 0, r == 0), 0.0, s_face)
        g = (
            jnp.maximum(e_face, 0.0), jnp.minimum(w_face, 0.0),
            jnp.maximum(n_face, 0.0), jnp.minimum(s_face, 0.0),
        )
        for k in range(4):
            gains[k, r] = g[k]
        for t in range(TR):
            acc[r, t * LEV : (t + 1) * LEV, :] += advected(0, r, t, halo0, g)
        return halo0

    row_id = iota((LANES, LANES), 0)
    eye = (row_id == iota((LANES, LANES), 1)).astype(F32).astype(BF16)
    cells = iota((ROWS, 2 * LANES), 1).astype(F32)
    clane = iota((16, LANES), 1)

    def place_group(blocks, tiles, fresh=False):
        parts = []
        for h in range(GROUP // 8):
            s = [tiles[h * 8 + k].astype(F32) for k in range(8)]
            parts.append(jnp.where(clane < 48, s[0], jnp.where(clane < 96, s[1], s[2])))
            parts.append(
                jnp.where(clane < 16, s[2], jnp.where(clane < 64, s[3], jnp.where(clane < 112, s[4], s[5])))
            )
            parts.append(jnp.where(clane < 32, s[5], jnp.where(clane < 80, s[6], s[7])))
        codes[...] = jnp.concatenate(parts, axis=1)
        shift = codes[pl.ds(core * 3, 1), :].astype(jnp.int32)
        lat_row = codes[pl.ds(core * 3 + 1, 1), :]
        lon_col = codes[pl.ds(core * 3 + 2, 1), :]
        turned = lax.dot_general(eye, blocks, (((1,), (1,)), ((), ())), preferred_element_type=F32)
        placed = []
        for t in range(TR):
            x = jnp.concatenate([turned[t * SPAN : (t + 1) * SPAN], jnp.zeros((8, ROWS), F32)], axis=0)
            for bit in (1, 2, 4):
                x = jnp.where(jnp.bitwise_and(shift, bit) != 0, pltpu.roll(x, bit, 0), x)
            x8 = jnp.concatenate([jnp.zeros((8, ROWS), F32), x[: LEV - 8]], axis=0)
            placed.append(jnp.where(jnp.bitwise_and(shift, 8) != 0, x8, x))
        placed = jnp.concatenate(placed, axis=0).astype(BF16)
        parity = jnp.bitwise_and(lat_row.astype(jnp.int32), 1).astype(F32)
        cell = jnp.broadcast_to(parity * LANES + lon_col, (8, ROWS))
        hot = jnp.where(jnp.transpose(cell)[:, 0:1] == cells, 1.0, 0.0).astype(BF16)
        for j in range(CLAT // 2):
            mine = jnp.where((lat_row == 2 * j) | (lat_row == 2 * j + 1), 1.0, 0.0).astype(BF16)
            res = jnp.dot(placed * mine, hot, preferred_element_type=F32)
            if fresh:
                acc[2 * j] = res[:, :LANES]
                acc[2 * j + 1] = res[:, LANES:]
            else:
                acc[2 * j] += res[:, :LANES]
                acc[2 * j + 1] += res[:, LANES:]

    mine_at = pl.ds(pl.multiple_of(core * CAP, 16), CAP)
    other_at = pl.ds(pl.multiple_of(CAP - core * CAP, 16), CAP)

    def forwards(g):
        at = pl.ds(g * GROUP, GROUP)
        return [
            pltpu.make_async_remote_copy(
                src_ref=recv.at[at, other_at, :], dst_ref=fwd.at[at],
                send_sem=fwd_send.at[0, g], recv_sem=fwd_recv.at[0, g],
                device_id=(sibling, lon), device_id_type=MESH,
            ),
            pltpu.make_async_remote_copy(
                src_ref=recv.at[at, 2 * CAP : BLOCK, :], dst_ref=fwdc.at[at],
                send_sem=fwd_send.at[1, g], recv_sem=fwd_recv.at[1, g],
                device_id=(sibling, lon), device_id_type=MESH,
            ),
        ]

    def arrived(g, lo):
        at = pl.ds(g * GROUP + lo, GROUP - lo)
        pltpu.make_async_remote_copy(
            src_ref=send.at[at], dst_ref=recv.at[at], send_sem=send_sem,
            recv_sem=recv_sem.at[g], device_id=(sibling, lon), device_id_type=MESH,
        ).wait_recv()

    def place_direct(g):
        at = pl.ds(g * GROUP, GROUP)
        place_group(recv[at, mine_at, :].reshape(ROWS, LANES), recv[at, 2 * CAP : BLOCK, :], g == 0)

    def place_forwarded(g):
        for copy in forwards(g):
            copy.wait_recv()
        at = pl.ds(g * GROUP, GROUP)
        place_group(fwd[at].reshape(ROWS, LANES), fwdc[at])

    own.wait()

    def take(g):
        arrived(g, 1 if g == 0 else 0)
        for copy in forwards(g):
            copy.start()
        place_direct(g)

    def finish_first():
        for copy in first_halo:
            copy.wait()
        lax.fori_loop(0, CLAT, first_row, merged(0), unroll=4)

    take(0)
    take(1)
    place_forwarded(0)
    take(2)
    place_forwarded(1)
    place_forwarded(2)
    take(3)
    finish_first()
    place_forwarded(3)

    edges[1] = column_step(1, lambda t, r: acc[r, t * LEV : (t + 1) * LEV, :])
    second_halo = halo_copies(1)
    for copy in second_halo:
        copy.start()
    for copy in second_halo:
        copy.wait()
    halo1 = merged(1)

    def second_row(r, carry):
        g = tuple(gains[k, r] for k in range(4))
        for t in range(TR):
            y = advected(1, r, t, halo1, g)
            out[pl.ds(t * LEV * CLAT + r, LEV, stride=CLAT), :] = y
            flux[pl.ds(t * CLAT + r, 1), :] = y[0:1] + acc[r, t * LEV : t * LEV + 1, :]
        return carry

    lax.fori_loop(0, CLAT, second_row, 0, unroll=4)
    for g in range(GROUPS):
        for copy in forwards(g):
            copy.wait_send()
    every = pl.ds(1, CHIPS - 1)
    pltpu.make_async_remote_copy(
        src_ref=send.at[every], dst_ref=recv.at[every], send_sem=send_sem,
        recv_sem=recv_sem.at[0], device_id=(sibling, lon), device_id_type=MESH,
    ).wait_send()


def local(adjoint_state, courant_east, courant_north, diffusion, convective_flux, convection,
          sounding_forcing, sounding_column, sounding_level, owner_counts):
    vmem = pl.BlockSpec(memory_space=pltpu.VMEM)
    dma = pltpu.SemaphoreType.DMA
    listed = sounding_forcing.shape[0]
    out, flux = pl.pallas_call(
        main_kernel,
        out_shape=(
            jax.ShapeDtypeStruct((TR * LEV * CLAT, LANES), F32),
            jax.ShapeDtypeStruct((TR * CLAT, LANES), F32),
        ),
        in_specs=[pl.BlockSpec(memory_space=pltpu.SMEM)] + [pl.BlockSpec(memory_space=pl.ANY)] * 9,
        out_specs=(vmem, vmem),
        scratch_shapes=[
            pltpu.VMEM((TR * LEV * CLAT, LANES), F32),
            pltpu.VMEM((LEV * CLAT, LANES), F32),
            pltpu.VMEM((LEV * CLAT, LANES), F32),
            pltpu.VMEM((CLAT, LANES), F32),
            pltpu.VMEM((CLAT, LANES), F32),
            pltpu.VMEM((LEV, LEV), F32),
            pltpu.VMEM((listed, LANES), BF16),
            pltpu.VMEM((listed // LANES, LANES), jnp.int32),
            pltpu.VMEM((listed // LANES, LANES), jnp.int32),
            pltpu.VMEM((listed, LANES), F32),
            pltpu.VMEM((56, LANES), jnp.int32),
            pltpu.SMEM((128,), jnp.int32),
            dma((9,)),
            pltpu.VMEM((CHIPS, BLOCK, LANES), BF16),
            pltpu.VMEM((CHIPS, BLOCK, LANES), BF16),
            pltpu.VMEM((CHIPS, CAP, LANES), BF16),
            pltpu.VMEM((CHIPS, 16, LANES), BF16),
            pltpu.VMEM((CLAT, TR * LEV, LANES), F32),
            pltpu.VMEM((2, CLAT + 2, TR * LEV, LANES), F32),
            pltpu.VMEM((4, CLAT, LEV, LANES), F32),
            pltpu.VMEM((256, LANES), F32),
            pltpu.VMEM((16, ROWS), F32),
            pltpu.VMEM((2, LEV, LANES), F32),
            pltpu.VMEM((2, LEV, LANES), F32),
            pltpu.VMEM((2, LEV, LANES), F32),
            pltpu.VMEM((LEV, LANES), F32),
            pltpu.VMEM((LEV, LANES), F32),
            dma,
            dma((GROUPS,)),
            dma((2, GROUPS)),
            dma((2, GROUPS)),
            dma((2, 5)),
            dma((2, 5)),
            dma,
        ],
        compiler_params=pltpu.CompilerParams(
            collective_id=0, has_side_effects=True, vmem_limit_bytes=60 << 20
        ),
        name="transport",
    )(
        owner_counts,
        adjoint_state.reshape(TR * LEV * CLAT, LANES),
        courant_east.reshape(LEV * CLAT, LANES),
        courant_north.reshape(LEV * CLAT, LANES),
        diffusion, convective_flux, convection,
        sounding_forcing,
        sounding_column.reshape(listed // LANES, LANES),
        sounding_level.reshape(listed // LANES, LANES),
    )
    return out.reshape(TR, LEV, CLAT, LANES), flux.reshape(TR, CLAT, LANES)


def solution(mesh):
    return jax.shard_map(
        local,
        mesh=mesh,
        in_specs=(
            P(None, None, "lat", "lon"),
            P(None, "lat", "lon"),
            P(None, "lat", "lon"),
            P("lat", "lon"),
            P("lat", "lon"),
            P(),
            P(("lat", "lon"), None),
            P(("lat", "lon")),
            P(("lat", "lon")),
            P(("lat", "lon"), None),
        ),
        out_specs=(P(None, None, "lat", "lon"), P(None, "lat", "lon")),
        check_vma=False,
    )
```

```python
import jax
import jax.numpy as jnp
from jax import lax
from jax.experimental import pallas as pl
from jax.experimental.pallas import tpu as pltpu
from jax.sharding import PartitionSpec as P

TR = 2
LEV = 72
SPAN = 64
CAP = 48
CLAT = 16
LANES = 128
CHIPS = 64
STRIDE = 45
TILES = CAP // 8
BLOCK = 2 * TILES + 1
GROUPS = ((0, 16), (16, 16), (32, 16), (48, 8), (56, 8))
F32 = jnp.float32
BF16 = jnp.bfloat16
COPIES = 4
MESH = pl.DeviceIdType.MESH


def place():
    lat = lax.axis_index("lat")
    lon = lax.axis_index("lon")
    return lat, lon, jnp.bitwise_and(lat, 1), jnp.right_shift(lat, 1) * 16 + lon


def peer_chip(chip, step):
    return jnp.bitwise_xor(chip, jnp.bitwise_and(step * STRIDE, CHIPS - 1))


def iota(shape, axis):
    return lax.broadcasted_iota(jnp.int32, shape, axis)


def main_kernel(
    counts, adj_hbm, ce_hbm, cn_hbm, dif_hbm, flx_hbm, conv_hbm, forcing_hbm, column_hbm, level_hbm,
    out, flux,
    adj, ce, cn, dif, flx, conv, forcing, column, level,
    rows_f32, targets, starts, load_sem,
    send, recv, fwd, fwdc, acc, field, gains, mixer, codes, edges, west_in, east_in, cn_edge, cn_south,
    send_sem, recv_sem, fwd_send, fwd_recv, halo_send, halo_recv, self_sem,
):
    lat, lon, core, chip = place()
    north = lax.rem(lat + 1, 8)
    south = lax.rem(lat + 7, 8)
    east = lax.rem(lon + 1, 16)
    west = lax.rem(lon + 15, 16)
    sibling = lat + 1 - 2 * core
    loads = [
        pltpu.make_async_copy(src, dst, load_sem.at[k])
        for k, (src, dst) in enumerate((
            (forcing_hbm, forcing), (column_hbm, column), (level_hbm, level), (adj_hbm, adj), (conv_hbm, conv),
            (dif_hbm, dif), (flx_hbm, flx), (ce_hbm, ce), (cn_hbm, cn),
        ))
    ]
    for copy in loads[:3]:
        copy.start()
    barrier = pltpu.get_barrier_semaphore()

    def peer(i):
        t = peer_chip(chip, i)
        return (jnp.right_shift(t, 4) * 2 + core, jnp.bitwise_and(t, 15))

    def greet(i, carry):
        pl.semaphore_signal(barrier, inc=1, device_id=peer(i), device_id_type=MESH)
        return carry

    lax.fori_loop(1, CHIPS, greet, 0, unroll=7)
    for other in (north, south):
        pl.semaphore_signal(barrier, inc=1, device_id=(other, lon), device_id_type=MESH)

    for copy in loads[3:]:
        copy.start()

    def prefix(o, total):
        starts[o] = total
        return total + counts[0, o]

    lax.fori_loop(0, 128, prefix, jnp.int32(0), unroll=8)
    for copy in loads[:3]:
        copy.wait()

    def widen(i, carry):
        at = pl.ds(pl.multiple_of(i * 256, 256), 256)
        rows_f32[at, :] = forcing[at, :].astype(F32)
        return carry

    lax.fori_loop(0, forcing.shape[0] // 256, widen, 0, unroll=2)
    targets[0:48, :] = level[...] * 2048 + column[...]
    targets[48:56, :] = jnp.zeros((8, LANES), jnp.int32)
    lane8 = iota((8, LANES), 1)
    sub8 = iota((8, LANES), 0)

    def pack(i):
        t = peer_chip(chip, i)
        first_lane = jnp.bitwise_and(i * CAP, LANES - 1)
        slot = jnp.bitwise_and(lane8 - first_lane, LANES - 1)
        tile = jnp.zeros((8, LANES), F32)
        for dc in range(2):
            owner = (jnp.right_shift(t, 4) * 2 + dc) * 16 + jnp.bitwise_and(t, 15)
            start = starts[owner]
            count = counts[0, owner]
            rows = rows_f32[pl.ds(start, CAP), :].reshape(TILES, 8, LANES)
            send[i, dc * TILES : (dc + 1) * TILES] = rows.astype(BF16)
            row = jnp.right_shift(start, 7)
            off = jnp.bitwise_and(start, LANES - 1)
            turn = jnp.bitwise_and(first_lane - off + LANES, LANES - 1)
            near = pltpu.roll(jnp.broadcast_to(targets[pl.ds(row, 1), :], (8, LANES)), turn, 1)
            far = pltpu.roll(jnp.broadcast_to(targets[pl.ds(row + 1, 1), :], (8, LANES)), turn, 1)
            code = jnp.where(slot < LANES - off, near, far)
            valid = slot < count
            shift = jnp.where(valid, jnp.right_shift(code, 11), 0)
            lat_row = jnp.where(valid, jnp.bitwise_and(jnp.right_shift(code, 7), 15), -1)
            lon_col = jnp.bitwise_and(code, 127)
            for k, part in enumerate((shift, lat_row, lon_col)):
                tile = jnp.where(sub8 == dc * 3 + k, part.astype(F32), tile)
        send[i, 2 * TILES] = tile.astype(BF16)

    def block_copy(i):
        return pltpu.make_async_remote_copy(
            src_ref=send.at[i], dst_ref=recv.at[i], send_sem=send_sem,
            recv_sem=recv_sem.at[jnp.where(i < 48, jnp.right_shift(i, 4), jnp.right_shift(i, 3) - 3)], device_id=peer(i), device_id_type=MESH,
        )

    pack(0)
    own = pltpu.make_async_copy(send.at[0], recv.at[0], self_sem)
    own.start()
    pl.semaphore_wait(barrier, CHIPS + 1)

    def post(i, carry):
        pack(i)
        block_copy(i).start()
        return carry

    lax.fori_loop(1, CHIPS, post, 0, unroll=3)
    for copy in loads[3:]:
        copy.wait()

    high = conv[...].astype(BF16).astype(F32)
    mixer[...] = jnp.zeros((256, LANES), F32)
    mixer[0:LEV, 0:LEV] = high
    mixer[LEV : 2 * LEV, 0:LEV] = high
    mixer[2 * LEV : 3 * LEV, 0:LEV] = conv[...] - high
    mix = jnp.transpose(mixer[...])[0:LEV].astype(BF16)
    lev2 = iota((LEV, 2 * LANES), 0)
    lane = iota((LEV, LANES), 1)

    def physics(x, f, d):
        x1 = x.astype(BF16).astype(F32)
        stack = jnp.concatenate([x1, x - x1, x1, jnp.zeros((40, 2 * LANES), F32)], axis=0)
        z = jnp.dot(mix, stack.astype(BF16), preferred_element_type=F32)
        m = x + f * z
        above = jnp.where(lev2 == LEV - 1, m, pltpu.roll(m, LEV - 1, 0))
        below = jnp.where(lev2 == 0, m, pltpu.roll(m, 1, 0))
        return m + d * (above - 2.0 * m + below)

    def column_step(e, load, after_edges):
        def pair(j, packed):
            r0 = 2 * j
            f = jnp.concatenate([flx[pl.ds(r0, 1), :], flx[pl.ds(r0 + 1, 1), :]], axis=1)
            d = jnp.concatenate([dif[pl.ds(r0, 1), :], dif[pl.ds(r0 + 1, 1), :]], axis=1)
            for t in range(TR):
                x = jnp.concatenate([load(t, r0), load(t, r0 + 1)], axis=1)
                y = physics(x, f, d)
                for k in range(2):
                    part = y[:, k * LANES : (k + 1) * LANES]
                    field[e, r0 + k + 1, t * LEV : (t + 1) * LEV, :] = part
                    at = 2 * (t * CLAT + r0 + k)
                    turned = pltpu.roll(part, at + 1, 1)
                    packed = jnp.where((lane == at) | (lane == at + 1), turned, packed)
            return packed

        packed = pair(CLAT // 2 - 1, pair(0, jnp.zeros((LEV, LANES), F32)))
        after_edges()
        return lax.fori_loop(1, CLAT // 2 - 1, pair, packed, unroll=6)

    def halo_copies(e):
        def rc(src, dst, k, dev):
            return pltpu.make_async_remote_copy(
                src_ref=src, dst_ref=dst, send_sem=halo_send.at[e, k],
                recv_sem=halo_recv.at[e, k], device_id=dev, device_id_type=MESH,
            )

        return [
            rc(edges.at[e], west_in.at[e], 0, (lat, east)),
            rc(edges.at[e], east_in.at[e], 1, (lat, west)),
            rc(field.at[e, CLAT], field.at[e, 0], 2, (north, lon)),
            rc(field.at[e, 1], field.at[e, CLAT + 1], 3, (south, lon)),
        ] + ([rc(cn_edge, cn_south, 4, (north, lon))] if e == 0 else [])

    def merged(e):
        return jnp.where(
            jnp.bitwise_and(lane, 1) == 0, west_in[e], pltpu.roll(east_in[e], LANES - 2, 1)
        )

    def advected(e, r, t, halo, g):
        at = 2 * (t * CLAT + r)
        turned = pltpu.roll(halo, lax.rem(2 * LANES - at, LANES), 1)
        rows = pl.ds(t * LEV, LEV)
        c = field[e, r + 1, rows, :]
        n = field[e, r + 2, rows, :]
        s = field[e, r, rows, :]
        ea = jnp.where(lane == LANES - 1, turned, pltpu.roll(c, LANES - 1, 1))
        we = jnp.where(lane == 0, turned, pltpu.roll(c, 1, 1))
        return c + g[0] * (ea - c) + g[1] * (c - we) + g[2] * (n - c) + g[3] * (c - s)

    packed = column_step(0, lambda t, r: adj[pl.ds(t * LEV * CLAT + r, LEV, stride=CLAT), :], lambda: None)

    def face_edge(r, packed):
        at = 64 + 2 * r
        turned = pltpu.roll(ce[pl.ds(r, LEV, stride=CLAT), :], at + 1, 1)
        return jnp.where(lane == at, turned, packed)

    edges[0] = lax.fori_loop(0, CLAT, face_edge, packed, unroll=True)
    cn_edge[...] = cn[pl.ds(CLAT - 1, LEV, stride=CLAT), :]
    first_halo = halo_copies(0)
    for copy in first_halo:
        copy.start()

    def first_row(r, halo0):
        e_face = ce[pl.ds(r, LEV, stride=CLAT), :]
        turned = pltpu.roll(halo0, lax.rem(2 * LANES - 64 - 2 * r, LANES), 1)
        w_face = jnp.where(lane == 0, turned, pltpu.roll(e_face, 1, 1))
        n_face = cn[pl.ds(r, LEV, stride=CLAT), :]
        top = jnp.logical_and(lat == 7, r == CLAT - 1)
        n_face = jnp.where(top, 0.0, n_face)
        s_face = jnp.where(r == 0, cn_south[...], cn[pl.ds(jnp.maximum(r - 1, 0), LEV, stride=CLAT), :])
        s_face = jnp.where(jnp.logical_and(lat == 0, r == 0), 0.0, s_face)
        g = (
            jnp.maximum(e_face, 0.0), jnp.minimum(w_face, 0.0),
            jnp.maximum(n_face, 0.0), jnp.minimum(s_face, 0.0),
        )
        for k in range(4):
            gains[k, r] = g[k]
        for t in range(TR):
            acc[r, t * LEV : (t + 1) * LEV, :] += advected(0, r, t, halo0, g)
        return halo0

    row_id = iota((LANES, LANES), 0)
    eye = (row_id == iota((LANES, LANES), 1)).astype(F32).astype(BF16)
    clane = iota((8, LANES), 1)

    def place_group(blocks, tiles, fresh=False):
        sources = blocks.shape[0]
        count = sources * CAP
        cells = iota((count, 2 * LANES), 1).astype(F32)
        blocks = blocks.astype(F32).reshape(count, LANES).astype(BF16)
        parts = []
        for h in range(sources // 8):
            s = [tiles[h * 8 + k].astype(F32) for k in range(8)]
            parts.append(jnp.where(clane < 48, s[0], jnp.where(clane < 96, s[1], s[2])))
            parts.append(
                jnp.where(clane < 16, s[2], jnp.where(clane < 64, s[3], jnp.where(clane < 112, s[4], s[5])))
            )
            parts.append(jnp.where(clane < 32, s[5], jnp.where(clane < 80, s[6], s[7])))
        codes[:, :count] = jnp.concatenate(parts, axis=1)
        shift = codes[pl.ds(core * 3, 1), :count].astype(jnp.int32)
        lat_row = codes[pl.ds(core * 3 + 1, 1), :count]
        lon_col = codes[pl.ds(core * 3 + 2, 1), :count]
        turned = lax.dot_general(eye, blocks, (((1,), (1,)), ((), ())), preferred_element_type=F32)
        placed = []
        for t in range(TR):
            x = jnp.concatenate([turned[t * SPAN : (t + 1) * SPAN], jnp.zeros((8, count), F32)], axis=0)
            for bit in (1, 2, 4):
                x = jnp.where(jnp.bitwise_and(shift, bit) != 0, pltpu.roll(x, bit, 0), x)
            x8 = jnp.concatenate([jnp.zeros((8, count), F32), x[: LEV - 8]], axis=0)
            placed.append(jnp.where(jnp.bitwise_and(shift, 8) != 0, x8, x))
        placed = jnp.concatenate(placed, axis=0).astype(BF16)
        parity = jnp.bitwise_and(lat_row.astype(jnp.int32), 1).astype(F32)
        cell = jnp.broadcast_to(parity * LANES + lon_col, (8, count))
        hot = jnp.where(jnp.transpose(cell)[:, 0:1] == cells, 1.0, 0.0).astype(BF16)
        for j in range(CLAT // 2):
            mine = jnp.where((lat_row == 2 * j) | (lat_row == 2 * j + 1), 1.0, 0.0).astype(BF16)
            res = jnp.dot(placed * mine, hot, preferred_element_type=F32)
            if fresh:
                acc[2 * j] = res[:, :LANES]
                acc[2 * j + 1] = res[:, LANES:]
            else:
                acc[2 * j] += res[:, :LANES]
                acc[2 * j + 1] += res[:, LANES:]

    mine_at = pl.ds(core * TILES, TILES)
    other_at = pl.ds(TILES - core * TILES, TILES)

    def forwards(g):
        at = pl.ds(*GROUPS[g])
        return [
            pltpu.make_async_remote_copy(
                src_ref=recv.at[at, other_at], dst_ref=fwd.at[at],
                send_sem=fwd_send.at[0, g], recv_sem=fwd_recv.at[0, g],
                device_id=(sibling, lon), device_id_type=MESH,
            ),
            pltpu.make_async_remote_copy(
                src_ref=recv.at[at, 2 * TILES], dst_ref=fwdc.at[at],
                send_sem=fwd_send.at[1, g], recv_sem=fwd_recv.at[1, g],
                device_id=(sibling, lon), device_id_type=MESH,
            ),
        ]

    def arrived(g, lo):
        at = pl.ds(GROUPS[g][0] + lo, GROUPS[g][1] - lo)
        pltpu.make_async_remote_copy(
            src_ref=send.at[at], dst_ref=recv.at[at], send_sem=send_sem,
            recv_sem=recv_sem.at[g], device_id=(sibling, lon), device_id_type=MESH,
        ).wait_recv()

    def place_direct(g):
        at = pl.ds(*GROUPS[g])
        place_group(recv[at, mine_at], recv[at, 2 * TILES], g == 0)

    def place_forwarded(g):
        for copy in forwards(g):
            copy.wait_recv()
        at = pl.ds(*GROUPS[g])
        place_group(fwd[at], fwdc[at])

    own.wait()

    def take(g):
        arrived(g, 1 if g == 0 else 0)
        for copy in forwards(g):
            copy.start()
        place_direct(g)

    def finish_first():
        for copy in first_halo:
            copy.wait()
        lax.fori_loop(0, CLAT, first_row, merged(0), unroll=4)

    take(0)
    take(1)
    place_forwarded(0)
    take(2)
    place_forwarded(1)
    place_forwarded(2)
    take(3)
    take(4)
    place_forwarded(3)
    finish_first()
    place_forwarded(4)

    second_halo = halo_copies(1)

    def planes():
        for copy in second_halo[2:]:
            copy.start()

    edges[1] = column_step(1, lambda t, r: acc[r, t * LEV : (t + 1) * LEV, :], planes)
    for copy in second_halo[:2]:
        copy.start()
    for copy in second_halo:
        copy.wait()
    halo1 = merged(1)

    def second_row(r, carry):
        g = tuple(gains[k, r] for k in range(4))
        for t in range(TR):
            y = advected(1, r, t, halo1, g)
            out[pl.ds(t * LEV * CLAT + r, LEV, stride=CLAT), :] = y
            flux[pl.ds(t * CLAT + r, 1), :] = y[0:1] + acc[r, t * LEV : t * LEV + 1, :]
        return carry

    lax.fori_loop(0, CLAT, second_row, 0, unroll=4)
    for g in range(len(GROUPS)):
        for copy in forwards(g):
            copy.wait_send()
    every = pl.ds(1, CHIPS - 1)
    pltpu.make_async_remote_copy(
        src_ref=send.at[every], dst_ref=recv.at[every], send_sem=send_sem,
        recv_sem=recv_sem.at[0], device_id=(sibling, lon), device_id_type=MESH,
    ).wait_send()


def finish_kernel(out_in, flux_in, out, flux, held, held_flux, sems):
    rows = TR * LEV * CLAT // COPIES
    parts = [(out_in, held, out, pl.ds(k * rows, rows)) for k in range(COPIES)]
    parts.append((flux_in, held_flux, flux, pl.ds(0, TR * CLAT)))
    loads, stores = [], []
    for k, (src, mid, dst, at) in enumerate(parts):
        loads.append(pltpu.make_async_copy(src.at[at], mid.at[at], sems.at[0, k]))
        stores.append(pltpu.make_async_copy(mid.at[at], dst.at[at], sems.at[1, k]))
    for copy in loads:
        copy.start()
    for load, store in zip(loads, stores):
        load.wait()
        store.start()
    for copy in stores:
        copy.wait()


def local(adjoint_state, courant_east, courant_north, diffusion, convective_flux, convection,
          sounding_forcing, sounding_column, sounding_level, owner_counts):
    vmem = pl.BlockSpec(memory_space=pltpu.VMEM)
    dma = pltpu.SemaphoreType.DMA
    listed = sounding_forcing.shape[0]
    out, flux = pl.pallas_call(
        main_kernel,
        out_shape=(
            jax.ShapeDtypeStruct((TR * LEV * CLAT, LANES), F32),
            jax.ShapeDtypeStruct((TR * CLAT, LANES), F32),
        ),
        in_specs=[pl.BlockSpec(memory_space=pltpu.SMEM)] + [pl.BlockSpec(memory_space=pl.ANY)] * 9,
        out_specs=(vmem, vmem),
        scratch_shapes=[
            pltpu.VMEM((TR * LEV * CLAT, LANES), F32),
            pltpu.VMEM((LEV * CLAT, LANES), F32),
            pltpu.VMEM((LEV * CLAT, LANES), F32),
            pltpu.VMEM((CLAT, LANES), F32),
            pltpu.VMEM((CLAT, LANES), F32),
            pltpu.VMEM((LEV, LEV), F32),
            pltpu.VMEM((listed, LANES), BF16),
            pltpu.VMEM((listed // LANES, LANES), jnp.int32),
            pltpu.VMEM((listed // LANES, LANES), jnp.int32),
            pltpu.VMEM((listed, LANES), F32),
            pltpu.VMEM((56, LANES), jnp.int32),
            pltpu.SMEM((128,), jnp.int32),
            dma((9,)),
            pltpu.VMEM((CHIPS, BLOCK, 8, LANES), BF16),
            pltpu.VMEM((CHIPS, BLOCK, 8, LANES), BF16),
            pltpu.VMEM((CHIPS, TILES, 8, LANES), BF16),
            pltpu.VMEM((CHIPS, 8, LANES), BF16),
            pltpu.VMEM((CLAT, TR * LEV, LANES), F32),
            pltpu.VMEM((2, CLAT + 2, TR * LEV, LANES), F32),
            pltpu.VMEM((4, CLAT, LEV, LANES), F32),
            pltpu.VMEM((256, LANES), F32),
            pltpu.VMEM((8, 16 * CAP), F32),
            pltpu.VMEM((2, LEV, LANES), F32),
            pltpu.VMEM((2, LEV, LANES), F32),
            pltpu.VMEM((2, LEV, LANES), F32),
            pltpu.VMEM((LEV, LANES), F32),
            pltpu.VMEM((LEV, LANES), F32),
            dma,
            dma((len(GROUPS),)),
            dma((2, len(GROUPS))),
            dma((2, len(GROUPS))),
            dma((2, 5)),
            dma((2, 5)),
            dma,
        ],
        compiler_params=pltpu.CompilerParams(
            collective_id=0, has_side_effects=True, vmem_limit_bytes=60 << 20
        ),
        name="transport",
    )(
        owner_counts,
        adjoint_state.reshape(TR * LEV * CLAT, LANES),
        courant_east.reshape(LEV * CLAT, LANES),
        courant_north.reshape(LEV * CLAT, LANES),
        diffusion, convective_flux, convection,
        sounding_forcing,
        sounding_column.reshape(listed // LANES, LANES),
        sounding_level.reshape(listed // LANES, LANES),
    )
    anywhere = pl.BlockSpec(memory_space=pl.ANY)
    out, flux = pl.pallas_call(
        finish_kernel,
        out_shape=(
            jax.ShapeDtypeStruct((TR * LEV * CLAT, LANES), F32),
            jax.ShapeDtypeStruct((TR * CLAT, LANES), F32),
        ),
        in_specs=[anywhere] * 2,
        out_specs=(anywhere, anywhere),
        scratch_shapes=[
            pltpu.VMEM((TR * LEV * CLAT, LANES), F32),
            pltpu.VMEM((TR * CLAT, LANES), F32),
            dma((2, COPIES + 1)),
        ],
        compiler_params=pltpu.CompilerParams(vmem_limit_bytes=60 << 20),
        name="finish",
    )(out, flux)
    return out.reshape(TR, LEV, CLAT, LANES), flux.reshape(TR, CLAT, LANES)


def solution(mesh):
    return jax.shard_map(
        local,
        mesh=mesh,
        in_specs=(
            P(None, None, "lat", "lon"),
            P(None, "lat", "lon"),
            P(None, "lat", "lon"),
            P("lat", "lon"),
            P("lat", "lon"),
            P(),
            P(("lat", "lon"), None),
            P(("lat", "lon")),
            P(("lat", "lon")),
            P(("lat", "lon"), None),
        ),
        out_specs=(P(None, None, "lat", "lon"), P(None, "lat", "lon")),
        check_vma=False,
    )
```

```python
import jax
import jax.numpy as jnp
from jax import lax
from jax.experimental import pallas as pl
from jax.experimental.pallas import tpu as pltpu
from jax.sharding import PartitionSpec as P

TR = 2
LEV = 72
SPAN = 64
CAP = 48
CLAT = 16
LANES = 128
CHIPS = 64
STRIDE = 27
TILES = CAP // 8
BLOCK = 2 * TILES + 1
GROUPS = ((0, 16), (16, 16), (32, 16), (48, 8), (56, 8))
F32 = jnp.float32
BF16 = jnp.bfloat16
COPIES = 4
MESH = pl.DeviceIdType.MESH


def place():
    lat = lax.axis_index("lat")
    lon = lax.axis_index("lon")
    return lat, lon, jnp.bitwise_and(lat, 1), jnp.right_shift(lat, 1) * 16 + lon


def peer_chip(chip, step):
    return jnp.bitwise_xor(chip, jnp.bitwise_and(step * STRIDE, CHIPS - 1))


def iota(shape, axis):
    return lax.broadcasted_iota(jnp.int32, shape, axis)


def main_kernel(
    counts, adj_hbm, ce_hbm, cn_hbm, dif_hbm, flx_hbm, conv_hbm, forcing_hbm, column_hbm, level_hbm,
    out_hbm, flux_hbm,
    out, flux, out_sem,
    adj, ce, cn, dif, flx, conv, forcing, column, level,
    rows_f32, targets, starts, load_sem,
    send, recv, fwd, acc, field, gains, mixer, codes, edges, west_in, east_in, cn_edge, cn_south,
    send_sem, recv_sem, fwd_send, fwd_recv, halo_send, halo_recv, self_sem,
):
    lat, lon, core, chip = place()
    north = lax.rem(lat + 1, 8)
    south = lax.rem(lat + 7, 8)
    east = lax.rem(lon + 1, 16)
    west = lax.rem(lon + 15, 16)
    sibling = lat + 1 - 2 * core
    loads = [
        pltpu.make_async_copy(src, dst, load_sem.at[k])
        for k, (src, dst) in enumerate((
            (forcing_hbm, forcing), (column_hbm, column), (level_hbm, level), (adj_hbm, adj), (conv_hbm, conv),
            (dif_hbm, dif), (flx_hbm, flx), (ce_hbm, ce), (cn_hbm, cn),
        ))
    ]
    for copy in loads[:3]:
        copy.start()
    barrier = pltpu.get_barrier_semaphore()

    def peer(i):
        t = peer_chip(chip, i)
        return (jnp.right_shift(t, 4) * 2 + core, jnp.bitwise_and(t, 15))

    def greet(i, carry):
        pl.semaphore_signal(barrier, inc=1, device_id=peer(i), device_id_type=MESH)
        return carry

    lax.fori_loop(1, CHIPS, greet, 0, unroll=7)
    for other in (north, south):
        pl.semaphore_signal(barrier, inc=1, device_id=(other, lon), device_id_type=MESH)

    for copy in loads[3:]:
        copy.start()

    def prefix(o, total):
        starts[o] = total
        return total + counts[0, o]

    lax.fori_loop(0, 128, prefix, jnp.int32(0), unroll=8)
    for copy in loads[:3]:
        copy.wait()

    def widen(i, carry):
        at = pl.ds(pl.multiple_of(i * 256, 256), 256)
        rows_f32[at, :] = forcing[at, :].astype(F32)
        return carry

    lax.fori_loop(0, forcing.shape[0] // 256, widen, 0, unroll=2)
    targets[0:48, :] = level[...] * 2048 + column[...]
    targets[48:56, :] = jnp.zeros((8, LANES), jnp.int32)
    lane8 = iota((8, LANES), 1)
    sub8 = iota((8, LANES), 0)

    def pack(i):
        t = peer_chip(chip, i)
        first_lane = jnp.bitwise_and(i * CAP, LANES - 1)
        slot = jnp.bitwise_and(lane8 - first_lane, LANES - 1)
        tile = jnp.zeros((8, LANES), F32)
        for dc in range(2):
            owner = (jnp.right_shift(t, 4) * 2 + dc) * 16 + jnp.bitwise_and(t, 15)
            start = starts[owner]
            count = counts[0, owner]
            rows = rows_f32[pl.ds(start, CAP), :].reshape(TILES, 8, LANES)
            at = dc * (TILES + 1)
            send[i, at : at + TILES] = rows.astype(BF16)
            row = jnp.right_shift(start, 7)
            off = jnp.bitwise_and(start, LANES - 1)
            turn = jnp.bitwise_and(first_lane - off + LANES, LANES - 1)
            near = pltpu.roll(jnp.broadcast_to(targets[pl.ds(row, 1), :], (8, LANES)), turn, 1)
            far = pltpu.roll(jnp.broadcast_to(targets[pl.ds(row + 1, 1), :], (8, LANES)), turn, 1)
            code = jnp.where(slot < LANES - off, near, far)
            valid = slot < count
            shift = jnp.where(valid, jnp.right_shift(code, 11), 0)
            lat_row = jnp.where(valid, jnp.bitwise_and(jnp.right_shift(code, 7), 15), -1)
            lon_col = jnp.bitwise_and(code, 127)
            for k, part in enumerate((shift, lat_row, lon_col)):
                tile = jnp.where(sub8 == dc * 3 + k, part.astype(F32), tile)
        send[i, TILES] = tile.astype(BF16)

    def block_copy(i):
        return pltpu.make_async_remote_copy(
            src_ref=send.at[i], dst_ref=recv.at[i], send_sem=send_sem,
            recv_sem=recv_sem.at[jnp.where(i < 48, jnp.right_shift(i, 4), jnp.right_shift(i, 3) - 3)], device_id=peer(i), device_id_type=MESH,
        )

    pack(0)
    own = pltpu.make_async_copy(send.at[0], recv.at[0], self_sem)
    own.start()
    pl.semaphore_wait(barrier, CHIPS + 1)

    def post(i, carry):
        pack(i)
        block_copy(i).start()
        return carry

    lax.fori_loop(1, CHIPS, post, 0, unroll=3)
    for copy in loads[3:]:
        copy.wait()

    high = conv[...].astype(BF16).astype(F32)
    mixer[...] = jnp.zeros((256, LANES), F32)
    mixer[0:LEV, 0:LEV] = high
    mixer[LEV : 2 * LEV, 0:LEV] = high
    mixer[2 * LEV : 3 * LEV, 0:LEV] = conv[...] - high
    mix = jnp.transpose(mixer[...])[0:LEV].astype(BF16)
    lev2 = iota((LEV, 2 * LANES), 0)
    lane = iota((LEV, LANES), 1)

    def physics(x, f, d):
        x1 = x.astype(BF16).astype(F32)
        stack = jnp.concatenate([x1, x - x1, x1, jnp.zeros((40, 2 * LANES), F32)], axis=0)
        z = jnp.dot(mix, stack.astype(BF16), preferred_element_type=F32)
        m = x + f * z
        above = jnp.where(lev2 == LEV - 1, m, pltpu.roll(m, LEV - 1, 0))
        below = jnp.where(lev2 == 0, m, pltpu.roll(m, 1, 0))
        return m + d * (above - 2.0 * m + below)

    def column_step(e, load, after_edges):
        def pair(j, packed):
            r0 = 2 * j
            f = jnp.concatenate([flx[pl.ds(r0, 1), :], flx[pl.ds(r0 + 1, 1), :]], axis=1)
            d = jnp.concatenate([dif[pl.ds(r0, 1), :], dif[pl.ds(r0 + 1, 1), :]], axis=1)
            for t in range(TR):
                x = jnp.concatenate([load(t, r0), load(t, r0 + 1)], axis=1)
                y = physics(x, f, d)
                for k in range(2):
                    part = y[:, k * LANES : (k + 1) * LANES]
                    field[e, r0 + k + 1, t * LEV : (t + 1) * LEV, :] = part
                    at = 2 * (t * CLAT + r0 + k)
                    turned = pltpu.roll(part, at + 1, 1)
                    packed = jnp.where((lane == at) | (lane == at + 1), turned, packed)
            return packed

        packed = pair(CLAT // 2 - 1, pair(0, jnp.zeros((LEV, LANES), F32)))
        after_edges()
        return lax.fori_loop(1, CLAT // 2 - 1, pair, packed, unroll=6)

    def halo_copies(e):
        def rc(src, dst, k, dev):
            return pltpu.make_async_remote_copy(
                src_ref=src, dst_ref=dst, send_sem=halo_send.at[e, k],
                recv_sem=halo_recv.at[e, k], device_id=dev, device_id_type=MESH,
            )

        return [
            rc(edges.at[e], west_in.at[e], 0, (lat, east)),
            rc(edges.at[e], east_in.at[e], 1, (lat, west)),
            rc(field.at[e, CLAT], field.at[e, 0], 2, (north, lon)),
            rc(field.at[e, 1], field.at[e, CLAT + 1], 3, (south, lon)),
        ] + ([rc(cn_edge, cn_south, 4, (north, lon))] if e == 0 else [])

    def merged(e):
        return jnp.where(
            jnp.bitwise_and(lane, 1) == 0, west_in[e], pltpu.roll(east_in[e], LANES - 2, 1)
        )

    def advected(e, r, t, halo, g):
        at = 2 * (t * CLAT + r)
        turned = pltpu.roll(halo, lax.rem(2 * LANES - at, LANES), 1)
        rows = pl.ds(t * LEV, LEV)
        c = field[e, r + 1, rows, :]
        n = field[e, r + 2, rows, :]
        s = field[e, r, rows, :]
        ea = jnp.where(lane == LANES - 1, turned, pltpu.roll(c, LANES - 1, 1))
        we = jnp.where(lane == 0, turned, pltpu.roll(c, 1, 1))
        return c + g[0] * (ea - c) + g[1] * (c - we) + g[2] * (n - c) + g[3] * (c - s)

    packed = column_step(0, lambda t, r: adj[pl.ds(t * LEV * CLAT + r, LEV, stride=CLAT), :], lambda: None)

    def face_edge(r, packed):
        at = 64 + 2 * r
        turned = pltpu.roll(ce[pl.ds(r, LEV, stride=CLAT), :], at + 1, 1)
        return jnp.where(lane == at, turned, packed)

    edges[0] = lax.fori_loop(0, CLAT, face_edge, packed, unroll=True)
    cn_edge[...] = cn[pl.ds(CLAT - 1, LEV, stride=CLAT), :]
    first_halo = halo_copies(0)
    for copy in first_halo:
        copy.start()

    def first_row(r, halo0):
        e_face = ce[pl.ds(r, LEV, stride=CLAT), :]
        turned = pltpu.roll(halo0, lax.rem(2 * LANES - 64 - 2 * r, LANES), 1)
        w_face = jnp.where(lane == 0, turned, pltpu.roll(e_face, 1, 1))
        n_face = cn[pl.ds(r, LEV, stride=CLAT), :]
        top = jnp.logical_and(lat == 7, r == CLAT - 1)
        n_face = jnp.where(top, 0.0, n_face)
        s_face = jnp.where(r == 0, cn_south[...], cn[pl.ds(jnp.maximum(r - 1, 0), LEV, stride=CLAT), :])
        s_face = jnp.where(jnp.logical_and(lat == 0, r == 0), 0.0, s_face)
        g = (
            jnp.maximum(e_face, 0.0), jnp.minimum(w_face, 0.0),
            jnp.maximum(n_face, 0.0), jnp.minimum(s_face, 0.0),
        )
        for k in range(4):
            gains[k, r] = g[k]
        for t in range(TR):
            acc[r, t * LEV : (t + 1) * LEV, :] += advected(0, r, t, halo0, g)
        return halo0

    row_id = iota((LANES, LANES), 0)
    eye = (row_id == iota((LANES, LANES), 1)).astype(F32).astype(BF16)
    clane = iota((8, LANES), 1)

    def place_group(blocks, tiles, fresh=False):
        sources = blocks.shape[0]
        count = sources * CAP
        cells = iota((count, 2 * LANES), 1).astype(F32)
        blocks = blocks.astype(F32).reshape(count, LANES).astype(BF16)
        parts = []
        for h in range(sources // 8):
            s = [tiles[h * 8 + k].astype(F32) for k in range(8)]
            parts.append(jnp.where(clane < 48, s[0], jnp.where(clane < 96, s[1], s[2])))
            parts.append(
                jnp.where(clane < 16, s[2], jnp.where(clane < 64, s[3], jnp.where(clane < 112, s[4], s[5])))
            )
            parts.append(jnp.where(clane < 32, s[5], jnp.where(clane < 80, s[6], s[7])))
        codes[:, :count] = jnp.concatenate(parts, axis=1)
        shift = codes[pl.ds(core * 3, 1), :count].astype(jnp.int32)
        lat_row = codes[pl.ds(core * 3 + 1, 1), :count]
        lon_col = codes[pl.ds(core * 3 + 2, 1), :count]
        turned = lax.dot_general(eye, blocks, (((1,), (1,)), ((), ())), preferred_element_type=F32)
        placed = []
        for t in range(TR):
            x = jnp.concatenate([turned[t * SPAN : (t + 1) * SPAN], jnp.zeros((8, count), F32)], axis=0)
            for bit in (1, 2, 4):
                x = jnp.where(jnp.bitwise_and(shift, bit) != 0, pltpu.roll(x, bit, 0), x)
            x8 = jnp.concatenate([jnp.zeros((8, count), F32), x[: LEV - 8]], axis=0)
            placed.append(jnp.where(jnp.bitwise_and(shift, 8) != 0, x8, x))
        placed = jnp.concatenate(placed, axis=0).astype(BF16)
        parity = jnp.bitwise_and(lat_row.astype(jnp.int32), 1).astype(F32)
        cell = jnp.broadcast_to(parity * LANES + lon_col, (8, count))
        hot = jnp.where(jnp.transpose(cell)[:, 0:1] == cells, 1.0, 0.0).astype(BF16)
        for j in range(CLAT // 2):
            mine = jnp.where((lat_row == 2 * j) | (lat_row == 2 * j + 1), 1.0, 0.0).astype(BF16)
            res = jnp.dot(placed * mine, hot, preferred_element_type=F32)
            if fresh:
                acc[2 * j] = res[:, :LANES]
                acc[2 * j + 1] = res[:, LANES:]
            else:
                acc[2 * j] += res[:, :LANES]
                acc[2 * j + 1] += res[:, LANES:]

    mine_at = pl.ds(core * (TILES + 1), TILES)
    other_at = pl.ds(TILES - core * TILES, TILES + 1)

    def forwards(g):
        at = pl.ds(*GROUPS[g])
        return [
            pltpu.make_async_remote_copy(
                src_ref=recv.at[at, other_at], dst_ref=fwd.at[at],
                send_sem=fwd_send.at[g], recv_sem=fwd_recv.at[g],
                device_id=(sibling, lon), device_id_type=MESH,
            )
        ]

    def arrived(g, lo):
        at = pl.ds(GROUPS[g][0] + lo, GROUPS[g][1] - lo)
        pltpu.make_async_remote_copy(
            src_ref=send.at[at], dst_ref=recv.at[at], send_sem=send_sem,
            recv_sem=recv_sem.at[g], device_id=(sibling, lon), device_id_type=MESH,
        ).wait_recv()

    def place_direct(g):
        at = pl.ds(*GROUPS[g])
        place_group(recv[at, mine_at], recv[at, TILES], g == 0)

    def place_forwarded(g):
        for copy in forwards(g):
            copy.wait_recv()
        at = pl.ds(*GROUPS[g])
        place_group(fwd[at, pl.ds(core, TILES)], fwd[at, TILES - core * TILES])

    own.wait()

    def take(g):
        arrived(g, 1 if g == 0 else 0)
        for copy in forwards(g):
            copy.start()
        place_direct(g)

    def finish_first():
        for copy in first_halo:
            copy.wait()
        lax.fori_loop(0, CLAT, first_row, merged(0), unroll=4)

    take(0)
    take(1)
    place_forwarded(0)
    take(2)
    place_forwarded(1)
    place_forwarded(2)
    take(3)
    take(4)
    place_forwarded(3)
    finish_first()
    place_forwarded(4)

    second_halo = halo_copies(1)

    def planes():
        for copy in second_halo[2:]:
            copy.start()

    edges[1] = column_step(1, lambda t, r: acc[r, t * LEV : (t + 1) * LEV, :], planes)
    for copy in second_halo[:2]:
        copy.start()
    def inner_row(r, carry):
        g = tuple(gains[k, r] for k in range(4))
        for t in range(TR):
            rows = pl.ds(t * LEV, LEV)
            c = field[1, r + 1, rows, :]
            n = field[1, r + 2, rows, :]
            s = field[1, r, rows, :]
            ea = jnp.where(lane == LANES - 1, 0.0, pltpu.roll(c, LANES - 1, 1))
            we = jnp.where(lane == 0, 0.0, pltpu.roll(c, 1, 1))
            out[pl.ds(t * LEV * CLAT + r, LEV, stride=CLAT), :] = (
                c + g[0] * (ea - c) + g[1] * (c - we) + g[2] * (n - c) + g[3] * (c - s)
            )
        return carry

    lax.fori_loop(1, CLAT - 1, inner_row, 0, unroll=7)
    for copy in second_halo:
        copy.wait()
    halo1 = merged(1)
    side = jnp.where(lane == LANES - 1, 1.0, 0.0)
    stores = []
    for t in range(TR):

        def finished(r, y, t=t):
            out[pl.ds(t * LEV * CLAT + r, LEV, stride=CLAT), :] = y
            flux[pl.ds(t * CLAT + r, 1), :] = y[0:1] + acc[r, t * LEV : t * LEV + 1, :]

        def outer_row(r, carry, t=t, finished=finished):
            at = 2 * (t * CLAT + r)
            turned = pltpu.roll(halo1, lax.rem(2 * LANES - at, LANES), 1)
            y = out[pl.ds(t * LEV * CLAT + r, LEV, stride=CLAT), :]
            finished(r, y + turned * jnp.where(lane == 0, -gains[1, r], side * gains[0, r]))
            return carry

        lax.fori_loop(1, CLAT - 1, outer_row, 0, unroll=7)
        for r in (0, CLAT - 1):
            g = tuple(gains[k, r] for k in range(4))
            finished(r, advected(1, r, t, halo1, g))
        at = pl.ds(t * LEV * CLAT, LEV * CLAT)
        stores.append(pltpu.make_async_copy(out.at[at], out_hbm.at[at], out_sem.at[t]))
        stores[-1].start()
    stores.append(pltpu.make_async_copy(flux, flux_hbm, out_sem.at[TR]))
    stores[-1].start()
    for g in range(len(GROUPS)):
        for copy in forwards(g):
            copy.wait_send()
    every = pl.ds(1, CHIPS - 1)
    pltpu.make_async_remote_copy(
        src_ref=send.at[every], dst_ref=recv.at[every], send_sem=send_sem,
        recv_sem=recv_sem.at[0], device_id=(sibling, lon), device_id_type=MESH,
    ).wait_send()
    for copy in stores:
        copy.wait()


def finish_kernel(out_in, flux_in, out, flux, held, held_flux, sems):
    rows = TR * LEV * CLAT // COPIES
    parts = [(out_in, held, out, pl.ds(k * rows, rows)) for k in range(COPIES)]
    parts.append((flux_in, held_flux, flux, pl.ds(0, TR * CLAT)))
    loads, stores = [], []
    for k, (src, mid, dst, at) in enumerate(parts):
        loads.append(pltpu.make_async_copy(src.at[at], mid.at[at], sems.at[0, k]))
        stores.append(pltpu.make_async_copy(mid.at[at], dst.at[at], sems.at[1, k]))
    for copy in loads:
        copy.start()
    for load, store in zip(loads, stores):
        load.wait()
        store.start()
    for copy in stores:
        copy.wait()


def local(adjoint_state, courant_east, courant_north, diffusion, convective_flux, convection,
          sounding_forcing, sounding_column, sounding_level, owner_counts):
    dma = pltpu.SemaphoreType.DMA
    listed = sounding_forcing.shape[0]
    out, flux = pl.pallas_call(
        main_kernel,
        out_shape=(
            jax.ShapeDtypeStruct((TR * LEV * CLAT, LANES), F32),
            jax.ShapeDtypeStruct((TR * CLAT, LANES), F32),
        ),
        in_specs=[pl.BlockSpec(memory_space=pltpu.SMEM)] + [pl.BlockSpec(memory_space=pl.ANY)] * 9,
        out_specs=(pl.BlockSpec(memory_space=pl.ANY), pl.BlockSpec(memory_space=pl.ANY)),
        scratch_shapes=[
            pltpu.VMEM((TR * LEV * CLAT, LANES), F32),
            pltpu.VMEM((TR * CLAT, LANES), F32),
            dma((TR + 1,)),
            pltpu.VMEM((TR * LEV * CLAT, LANES), F32),
            pltpu.VMEM((LEV * CLAT, LANES), F32),
            pltpu.VMEM((LEV * CLAT, LANES), F32),
            pltpu.VMEM((CLAT, LANES), F32),
            pltpu.VMEM((CLAT, LANES), F32),
            pltpu.VMEM((LEV, LEV), F32),
            pltpu.VMEM((listed, LANES), BF16),
            pltpu.VMEM((listed // LANES, LANES), jnp.int32),
            pltpu.VMEM((listed // LANES, LANES), jnp.int32),
            pltpu.VMEM((listed, LANES), F32),
            pltpu.VMEM((56, LANES), jnp.int32),
            pltpu.SMEM((128,), jnp.int32),
            dma((9,)),
            pltpu.VMEM((CHIPS, BLOCK, 8, LANES), BF16),
            pltpu.VMEM((CHIPS, BLOCK, 8, LANES), BF16),
            pltpu.VMEM((CHIPS, TILES + 1, 8, LANES), BF16),
            pltpu.VMEM((CLAT, TR * LEV, LANES), F32),
            pltpu.VMEM((2, CLAT + 2, TR * LEV, LANES), F32),
            pltpu.VMEM((4, CLAT, LEV, LANES), F32),
            pltpu.VMEM((256, LANES), F32),
            pltpu.VMEM((8, 16 * CAP), F32),
            pltpu.VMEM((2, LEV, LANES), F32),
            pltpu.VMEM((2, LEV, LANES), F32),
            pltpu.VMEM((2, LEV, LANES), F32),
            pltpu.VMEM((LEV, LANES), F32),
            pltpu.VMEM((LEV, LANES), F32),
            dma,
            dma((len(GROUPS),)),
            dma((len(GROUPS),)),
            dma((len(GROUPS),)),
            dma((2, 5)),
            dma((2, 5)),
            dma,
        ],
        compiler_params=pltpu.CompilerParams(
            collective_id=0, has_side_effects=True, vmem_limit_bytes=60 << 20
        ),
        name="transport",
    )(
        owner_counts,
        adjoint_state.reshape(TR * LEV * CLAT, LANES),
        courant_east.reshape(LEV * CLAT, LANES),
        courant_north.reshape(LEV * CLAT, LANES),
        diffusion, convective_flux, convection,
        sounding_forcing,
        sounding_column.reshape(listed // LANES, LANES),
        sounding_level.reshape(listed // LANES, LANES),
    )
    anywhere = pl.BlockSpec(memory_space=pl.ANY)
    out, flux = pl.pallas_call(
        finish_kernel,
        out_shape=(
            jax.ShapeDtypeStruct((TR * LEV * CLAT, LANES), F32),
            jax.ShapeDtypeStruct((TR * CLAT, LANES), F32),
        ),
        in_specs=[anywhere] * 2,
        out_specs=(anywhere, anywhere),
        scratch_shapes=[
            pltpu.VMEM((TR * LEV * CLAT, LANES), F32),
            pltpu.VMEM((TR * CLAT, LANES), F32),
            dma((2, COPIES + 1)),
        ],
        compiler_params=pltpu.CompilerParams(vmem_limit_bytes=60 << 20),
        name="finish",
    )(out, flux)
    return out.reshape(TR, LEV, CLAT, LANES), flux.reshape(TR, CLAT, LANES)


def solution(mesh):
    return jax.shard_map(
        local,
        mesh=mesh,
        in_specs=(
            P(None, None, "lat", "lon"),
            P(None, "lat", "lon"),
            P(None, "lat", "lon"),
            P("lat", "lon"),
            P("lat", "lon"),
            P(),
            P(("lat", "lon"), None),
            P(("lat", "lon")),
            P(("lat", "lon")),
            P(("lat", "lon"), None),
        ),
        out_specs=(P(None, None, "lat", "lon"), P(None, "lat", "lon")),
        check_vma=False,
    )
```

```python
import jax
import jax.numpy as jnp
from jax import lax
from jax.experimental import pallas as pl
from jax.experimental.pallas import tpu as pltpu
from jax.sharding import PartitionSpec as P

TR = 2
LEV = 72
SPAN = 64
CAP = 48
CLAT = 16
LANES = 128
CHIPS = 64
STRIDE = 27
TILES = CAP // 8
BLOCK = 2 * TILES + 1
GROUPS = ((0, 16), (16, 16), (32, 16), (48, 8), (56, 8))
F32 = jnp.float32
BF16 = jnp.bfloat16
COPIES = 4
MESH = pl.DeviceIdType.MESH


def place():
    lat = lax.axis_index("lat")
    lon = lax.axis_index("lon")
    return lat, lon, jnp.bitwise_and(lat, 1), jnp.right_shift(lat, 1) * 16 + lon


def peer_chip(chip, step):
    return jnp.bitwise_xor(chip, jnp.bitwise_and(step * STRIDE, CHIPS - 1))


def iota(shape, axis):
    return lax.broadcasted_iota(jnp.int32, shape, axis)


def main_kernel(
    counts, adj_hbm, ce_hbm, cn_hbm, dif_hbm, flx_hbm, conv_hbm, forcing_hbm, column_hbm, level_hbm,
    out_hbm, flux_hbm,
    out, flux, out_sem,
    adj, ce, cn, dif, flx, conv, forcing, column, level,
    rows_f32, targets, starts, load_sem,
    send, recv, fwd, acc, field, gains, mixer, codes, edges, west_in, east_in, cn_edge, cn_south,
    send_sem, recv_sem, fwd_send, fwd_recv, halo_send, halo_recv, self_sem,
):
    lat, lon, core, chip = place()
    north = lax.rem(lat + 1, 8)
    south = lax.rem(lat + 7, 8)
    east = lax.rem(lon + 1, 16)
    west = lax.rem(lon + 15, 16)
    sibling = lat + 1 - 2 * core
    loads = [
        pltpu.make_async_copy(src, dst, load_sem.at[k])
        for k, (src, dst) in enumerate((
            (forcing_hbm, forcing), (column_hbm, column), (level_hbm, level), (adj_hbm, adj), (conv_hbm, conv),
            (dif_hbm, dif), (flx_hbm, flx), (ce_hbm, ce), (cn_hbm, cn),
        ))
    ]
    for copy in loads[:3]:
        copy.start()
    barrier = pltpu.get_barrier_semaphore()

    def peer(i):
        t = peer_chip(chip, i)
        return (jnp.right_shift(t, 4) * 2 + core, jnp.bitwise_and(t, 15))

    def greet(i, carry):
        pl.semaphore_signal(barrier, inc=1, device_id=peer(i), device_id_type=MESH)
        return carry

    lax.fori_loop(1, CHIPS, greet, 0, unroll=7)
    for other in (north, south):
        pl.semaphore_signal(barrier, inc=1, device_id=(other, lon), device_id_type=MESH)

    for copy in loads[3:]:
        copy.start()

    def prefix(o, total):
        starts[o] = total
        return total + counts[0, o]

    lax.fori_loop(0, 128, prefix, jnp.int32(0), unroll=8)
    for copy in loads[:3]:
        copy.wait()

    def widen(i, carry):
        at = pl.ds(pl.multiple_of(i * 256, 256), 256)
        rows_f32[at, :] = forcing[at, :].astype(F32)
        return carry

    lax.fori_loop(0, forcing.shape[0] // 256, widen, 0, unroll=2)
    targets[0:48, :] = level[...] * 2048 + column[...]
    targets[48:56, :] = jnp.zeros((8, LANES), jnp.int32)
    lane8 = iota((8, LANES), 1)
    sub8 = iota((8, LANES), 0)

    def pack(i):
        t = peer_chip(chip, i)
        first_lane = jnp.bitwise_and(i * CAP, LANES - 1)
        slot = jnp.bitwise_and(lane8 - first_lane, LANES - 1)
        tile = jnp.zeros((8, LANES), F32)
        for dc in range(2):
            owner = (jnp.right_shift(t, 4) * 2 + dc) * 16 + jnp.bitwise_and(t, 15)
            start = starts[owner]
            count = counts[0, owner]
            rows = rows_f32[pl.ds(start, CAP), :].reshape(TILES, 8, LANES)
            at = dc * (TILES + 1)
            send[i, at : at + TILES] = rows.astype(BF16)
            row = jnp.right_shift(start, 7)
            off = jnp.bitwise_and(start, LANES - 1)
            turn = jnp.bitwise_and(first_lane - off + LANES, LANES - 1)
            near = pltpu.roll(jnp.broadcast_to(targets[pl.ds(row, 1), :], (8, LANES)), turn, 1)
            far = pltpu.roll(jnp.broadcast_to(targets[pl.ds(row + 1, 1), :], (8, LANES)), turn, 1)
            code = jnp.where(slot < LANES - off, near, far)
            valid = slot < count
            shift = jnp.where(valid, jnp.right_shift(code, 11), 0)
            lat_row = jnp.where(valid, jnp.bitwise_and(jnp.right_shift(code, 7), 15), -1)
            lon_col = jnp.bitwise_and(code, 127)
            for k, part in enumerate((shift, lat_row, lon_col)):
                tile = jnp.where(sub8 == dc * 3 + k, part.astype(F32), tile)
        send[i, TILES] = tile.astype(BF16)

    def block_copy(i):
        return pltpu.make_async_remote_copy(
            src_ref=send.at[i], dst_ref=recv.at[i], send_sem=send_sem,
            recv_sem=recv_sem.at[jnp.where(i < 48, jnp.right_shift(i, 4), jnp.right_shift(i, 3) - 3)], device_id=peer(i), device_id_type=MESH,
        )

    pack(0)
    pack(1)
    own = pltpu.make_async_copy(send.at[0], recv.at[0], self_sem)
    own.start()
    pl.semaphore_wait(barrier, CHIPS + 1)

    def post(i, carry):
        block_copy(i).start()
        pack(i + 1)
        return carry

    lax.fori_loop(1, CHIPS - 1, post, 0, unroll=2)
    block_copy(CHIPS - 1).start()
    for copy in loads[3:]:
        copy.wait()

    high = conv[...].astype(BF16).astype(F32)
    mixer[...] = jnp.zeros((256, LANES), F32)
    mixer[0:LEV, 0:LEV] = high
    mixer[LEV : 2 * LEV, 0:LEV] = high
    mixer[2 * LEV : 3 * LEV, 0:LEV] = conv[...] - high
    mix = jnp.transpose(mixer[...])[0:LEV].astype(BF16)
    lev2 = iota((LEV, 2 * LANES), 0)
    lane = iota((LEV, LANES), 1)

    def physics(x, f, d):
        x1 = x.astype(BF16).astype(F32)
        stack = jnp.concatenate([x1, x - x1, x1, jnp.zeros((40, 2 * LANES), F32)], axis=0)
        z = jnp.dot(mix, stack.astype(BF16), preferred_element_type=F32)
        m = x + f * z
        above = jnp.where(lev2 == LEV - 1, m, pltpu.roll(m, LEV - 1, 0))
        below = jnp.where(lev2 == 0, m, pltpu.roll(m, 1, 0))
        return m + d * (above - 2.0 * m + below)

    def column_step(e, load, after_edges):
        def pair(j, packed):
            r0 = 2 * j
            f = jnp.concatenate([flx[pl.ds(r0, 1), :], flx[pl.ds(r0 + 1, 1), :]], axis=1)
            d = jnp.concatenate([dif[pl.ds(r0, 1), :], dif[pl.ds(r0 + 1, 1), :]], axis=1)
            for t in range(TR):
                x = jnp.concatenate([load(t, r0), load(t, r0 + 1)], axis=1)
                y = physics(x, f, d)
                for k in range(2):
                    part = y[:, k * LANES : (k + 1) * LANES]
                    field[e, r0 + k + 1, t * LEV : (t + 1) * LEV, :] = part
                    at = 2 * (t * CLAT + r0 + k)
                    turned = pltpu.roll(part, at + 1, 1)
                    packed = jnp.where((lane == at) | (lane == at + 1), turned, packed)
            return packed

        packed = pair(CLAT // 2 - 1, pair(0, jnp.zeros((LEV, LANES), F32)))
        after_edges()
        return lax.fori_loop(1, CLAT // 2 - 1, pair, packed, unroll=6)

    def halo_copies(e):
        def rc(src, dst, k, dev):
            return pltpu.make_async_remote_copy(
                src_ref=src, dst_ref=dst, send_sem=halo_send.at[e, k],
                recv_sem=halo_recv.at[e, k], device_id=dev, device_id_type=MESH,
            )

        return [
            rc(edges.at[e], west_in.at[e], 0, (lat, east)),
            rc(edges.at[e], east_in.at[e], 1, (lat, west)),
            rc(field.at[e, CLAT], field.at[e, 0], 2, (north, lon)),
            rc(field.at[e, 1], field.at[e, CLAT + 1], 3, (south, lon)),
        ] + ([rc(cn_edge, cn_south, 4, (north, lon))] if e == 0 else [])

    def merged(e):
        return jnp.where(
            jnp.bitwise_and(lane, 1) == 0, west_in[e], pltpu.roll(east_in[e], LANES - 2, 1)
        )

    def advected(e, r, t, halo, g):
        at = 2 * (t * CLAT + r)
        turned = pltpu.roll(halo, lax.rem(2 * LANES - at, LANES), 1)
        rows = pl.ds(t * LEV, LEV)
        c = field[e, r + 1, rows, :]
        n = field[e, r + 2, rows, :]
        s = field[e, r, rows, :]
        ea = jnp.where(lane == LANES - 1, turned, pltpu.roll(c, LANES - 1, 1))
        we = jnp.where(lane == 0, turned, pltpu.roll(c, 1, 1))
        return c + g[0] * (ea - c) + g[1] * (c - we) + g[2] * (n - c) + g[3] * (c - s)

    packed = column_step(0, lambda t, r: adj[pl.ds(t * LEV * CLAT + r, LEV, stride=CLAT), :], lambda: None)

    def face_edge(r, packed):
        at = 64 + 2 * r
        turned = pltpu.roll(ce[pl.ds(r, LEV, stride=CLAT), :], at + 1, 1)
        return jnp.where(lane == at, turned, packed)

    edges[0] = lax.fori_loop(0, CLAT, face_edge, packed, unroll=True)
    cn_edge[...] = cn[pl.ds(CLAT - 1, LEV, stride=CLAT), :]
    first_halo = halo_copies(0)
    for copy in first_halo:
        copy.start()

    def first_row(r, halo0):
        e_face = ce[pl.ds(r, LEV, stride=CLAT), :]
        turned = pltpu.roll(halo0, lax.rem(2 * LANES - 64 - 2 * r, LANES), 1)
        w_face = jnp.where(lane == 0, turned, pltpu.roll(e_face, 1, 1))
        n_face = cn[pl.ds(r, LEV, stride=CLAT), :]
        top = jnp.logical_and(lat == 7, r == CLAT - 1)
        n_face = jnp.where(top, 0.0, n_face)
        s_face = jnp.where(r == 0, cn_south[...], cn[pl.ds(jnp.maximum(r - 1, 0), LEV, stride=CLAT), :])
        s_face = jnp.where(jnp.logical_and(lat == 0, r == 0), 0.0, s_face)
        g = (
            jnp.maximum(e_face, 0.0), jnp.minimum(w_face, 0.0),
            jnp.maximum(n_face, 0.0), jnp.minimum(s_face, 0.0),
        )
        for k in range(4):
            gains[k, r] = g[k]
        for t in range(TR):
            acc[r, t * LEV : (t + 1) * LEV, :] += advected(0, r, t, halo0, g)
        return halo0

    row_id = iota((LANES, LANES), 0)
    eye = (row_id == iota((LANES, LANES), 1)).astype(F32).astype(BF16)
    clane = iota((8, LANES), 1)

    def place_group(blocks, tiles, fresh=False):
        sources = blocks.shape[0]
        count = sources * CAP
        cells = iota((count, 2 * LANES), 1).astype(F32)
        blocks = blocks.astype(F32).reshape(count, LANES).astype(BF16)
        parts = []
        for h in range(sources // 8):
            s = [tiles[h * 8 + k].astype(F32) for k in range(8)]
            parts.append(jnp.where(clane < 48, s[0], jnp.where(clane < 96, s[1], s[2])))
            parts.append(
                jnp.where(clane < 16, s[2], jnp.where(clane < 64, s[3], jnp.where(clane < 112, s[4], s[5])))
            )
            parts.append(jnp.where(clane < 32, s[5], jnp.where(clane < 80, s[6], s[7])))
        codes[:, :count] = jnp.concatenate(parts, axis=1)
        shift = codes[pl.ds(core * 3, 1), :count].astype(jnp.int32)
        lat_row = codes[pl.ds(core * 3 + 1, 1), :count]
        lon_col = codes[pl.ds(core * 3 + 2, 1), :count]
        turned = lax.dot_general(eye, blocks, (((1,), (1,)), ((), ())), preferred_element_type=F32)
        placed = []
        for t in range(TR):
            x = jnp.concatenate([turned[t * SPAN : (t + 1) * SPAN], jnp.zeros((8, count), F32)], axis=0)
            for bit in (1, 2, 4):
                x = jnp.where(jnp.bitwise_and(shift, bit) != 0, pltpu.roll(x, bit, 0), x)
            x8 = jnp.concatenate([jnp.zeros((8, count), F32), x[: LEV - 8]], axis=0)
            placed.append(jnp.where(jnp.bitwise_and(shift, 8) != 0, x8, x))
        placed = jnp.concatenate(placed, axis=0).astype(BF16)
        parity = jnp.bitwise_and(lat_row.astype(jnp.int32), 1).astype(F32)
        cell = jnp.broadcast_to(parity * LANES + lon_col, (8, count))
        hot = jnp.where(jnp.transpose(cell)[:, 0:1] == cells, 1.0, 0.0).astype(BF16)
        for j in range(CLAT // 2):
            mine = jnp.where((lat_row == 2 * j) | (lat_row == 2 * j + 1), 1.0, 0.0).astype(BF16)
            res = jnp.dot(placed * mine, hot, preferred_element_type=F32)
            if fresh:
                acc[2 * j] = res[:, :LANES]
                acc[2 * j + 1] = res[:, LANES:]
            else:
                acc[2 * j] += res[:, :LANES]
                acc[2 * j + 1] += res[:, LANES:]

    mine_at = pl.ds(core * (TILES + 1), TILES)
    other_at = pl.ds(TILES - core * TILES, TILES + 1)

    def forwards(g):
        at = pl.ds(*GROUPS[g])
        return [
            pltpu.make_async_remote_copy(
                src_ref=recv.at[at, other_at], dst_ref=fwd.at[at],
                send_sem=fwd_send.at[g], recv_sem=fwd_recv.at[g],
                device_id=(sibling, lon), device_id_type=MESH,
            )
        ]

    def arrived(g, lo):
        at = pl.ds(GROUPS[g][0] + lo, GROUPS[g][1] - lo)
        pltpu.make_async_remote_copy(
            src_ref=send.at[at], dst_ref=recv.at[at], send_sem=send_sem,
            recv_sem=recv_sem.at[g], device_id=(sibling, lon), device_id_type=MESH,
        ).wait_recv()

    def place_direct(g):
        at = pl.ds(*GROUPS[g])
        place_group(recv[at, mine_at], recv[at, TILES], g == 0)

    def place_forwarded(g):
        for copy in forwards(g):
            copy.wait_recv()
        at = pl.ds(*GROUPS[g])
        place_group(fwd[at, pl.ds(core, TILES)], fwd[at, TILES - core * TILES])

    own.wait()

    def take(g):
        arrived(g, 1 if g == 0 else 0)
        for copy in forwards(g):
            copy.start()
        place_direct(g)

    def finish_first():
        for copy in first_halo:
            copy.wait()
        lax.fori_loop(0, CLAT, first_row, merged(0), unroll=4)

    take(0)
    take(1)
    place_forwarded(0)
    take(2)
    place_forwarded(1)
    place_forwarded(2)
    take(3)
    take(4)
    place_forwarded(3)
    finish_first()
    place_forwarded(4)

    second_halo = halo_copies(1)

    def planes():
        for copy in second_halo[2:]:
            copy.start()

    edges[1] = column_step(1, lambda t, r: acc[r, t * LEV : (t + 1) * LEV, :], planes)
    for copy in second_halo[:2]:
        copy.start()
    def inner_row(r, carry):
        g = tuple(gains[k, r] for k in range(4))
        for t in range(TR):
            rows = pl.ds(t * LEV, LEV)
            c = field[1, r + 1, rows, :]
            n = field[1, r + 2, rows, :]
            s = field[1, r, rows, :]
            ea = jnp.where(lane == LANES - 1, 0.0, pltpu.roll(c, LANES - 1, 1))
            we = jnp.where(lane == 0, 0.0, pltpu.roll(c, 1, 1))
            out[pl.ds(t * LEV * CLAT + r, LEV, stride=CLAT), :] = (
                c + g[0] * (ea - c) + g[1] * (c - we) + g[2] * (n - c) + g[3] * (c - s)
            )
        return carry

    lax.fori_loop(1, CLAT - 1, inner_row, 0, unroll=7)
    for copy in second_halo:
        copy.wait()
    halo1 = merged(1)
    side = jnp.where(lane == LANES - 1, 1.0, 0.0)
    stores = []
    for t in range(TR):

        def finished(r, y, t=t):
            out[pl.ds(t * LEV * CLAT + r, LEV, stride=CLAT), :] = y
            flux[pl.ds(t * CLAT + r, 1), :] = y[0:1] + acc[r, t * LEV : t * LEV + 1, :]

        def outer_row(r, carry, t=t, finished=finished):
            at = 2 * (t * CLAT + r)
            turned = pltpu.roll(halo1, lax.rem(2 * LANES - at, LANES), 1)
            y = out[pl.ds(t * LEV * CLAT + r, LEV, stride=CLAT), :]
            finished(r, y + turned * jnp.where(lane == 0, -gains[1, r], side * gains[0, r]))
            return carry

        lax.fori_loop(1, CLAT - 1, outer_row, 0, unroll=7)
        for r in (0, CLAT - 1):
            g = tuple(gains[k, r] for k in range(4))
            finished(r, advected(1, r, t, halo1, g))
        at = pl.ds(t * LEV * CLAT, LEV * CLAT)
        stores.append(pltpu.make_async_copy(out.at[at], out_hbm.at[at], out_sem.at[t]))
        stores[-1].start()
    stores.append(pltpu.make_async_copy(flux, flux_hbm, out_sem.at[TR]))
    stores[-1].start()
    for g in range(len(GROUPS)):
        for copy in forwards(g):
            copy.wait_send()
    every = pl.ds(1, CHIPS - 1)
    pltpu.make_async_remote_copy(
        src_ref=send.at[every], dst_ref=recv.at[every], send_sem=send_sem,
        recv_sem=recv_sem.at[0], device_id=(sibling, lon), device_id_type=MESH,
    ).wait_send()
    for copy in stores:
        copy.wait()


def finish_kernel(out_in, flux_in, out, flux, held, held_flux, sems):
    rows = TR * LEV * CLAT // COPIES
    parts = [(out_in, held, out, pl.ds(k * rows, rows)) for k in range(COPIES)]
    parts.append((flux_in, held_flux, flux, pl.ds(0, TR * CLAT)))
    loads, stores = [], []
    for k, (src, mid, dst, at) in enumerate(parts):
        loads.append(pltpu.make_async_copy(src.at[at], mid.at[at], sems.at[0, k]))
        stores.append(pltpu.make_async_copy(mid.at[at], dst.at[at], sems.at[1, k]))
    for copy in loads:
        copy.start()
    for load, store in zip(loads, stores):
        load.wait()
        store.start()
    for copy in stores:
        copy.wait()


def local(adjoint_state, courant_east, courant_north, diffusion, convective_flux, convection,
          sounding_forcing, sounding_column, sounding_level, owner_counts):
    dma = pltpu.SemaphoreType.DMA
    listed = sounding_forcing.shape[0]
    out, flux = pl.pallas_call(
        main_kernel,
        out_shape=(
            jax.ShapeDtypeStruct((TR * LEV * CLAT, LANES), F32),
            jax.ShapeDtypeStruct((TR * CLAT, LANES), F32),
        ),
        in_specs=[pl.BlockSpec(memory_space=pltpu.SMEM)] + [pl.BlockSpec(memory_space=pl.ANY)] * 9,
        out_specs=(pl.BlockSpec(memory_space=pl.ANY), pl.BlockSpec(memory_space=pl.ANY)),
        scratch_shapes=[
            pltpu.VMEM((TR * LEV * CLAT, LANES), F32),
            pltpu.VMEM((TR * CLAT, LANES), F32),
            dma((TR + 1,)),
            pltpu.VMEM((TR * LEV * CLAT, LANES), F32),
            pltpu.VMEM((LEV * CLAT, LANES), F32),
            pltpu.VMEM((LEV * CLAT, LANES), F32),
            pltpu.VMEM((CLAT, LANES), F32),
            pltpu.VMEM((CLAT, LANES), F32),
            pltpu.VMEM((LEV, LEV), F32),
            pltpu.VMEM((listed, LANES), BF16),
            pltpu.VMEM((listed // LANES, LANES), jnp.int32),
            pltpu.VMEM((listed // LANES, LANES), jnp.int32),
            pltpu.VMEM((listed, LANES), F32),
            pltpu.VMEM((56, LANES), jnp.int32),
            pltpu.SMEM((128,), jnp.int32),
            dma((9,)),
            pltpu.VMEM((CHIPS, BLOCK, 8, LANES), BF16),
            pltpu.VMEM((CHIPS, BLOCK, 8, LANES), BF16),
            pltpu.VMEM((CHIPS, TILES + 1, 8, LANES), BF16),
            pltpu.VMEM((CLAT, TR * LEV, LANES), F32),
            pltpu.VMEM((2, CLAT + 2, TR * LEV, LANES), F32),
            pltpu.VMEM((4, CLAT, LEV, LANES), F32),
            pltpu.VMEM((256, LANES), F32),
            pltpu.VMEM((8, 16 * CAP), F32),
            pltpu.VMEM((2, LEV, LANES), F32),
            pltpu.VMEM((2, LEV, LANES), F32),
            pltpu.VMEM((2, LEV, LANES), F32),
            pltpu.VMEM((LEV, LANES), F32),
            pltpu.VMEM((LEV, LANES), F32),
            dma,
            dma((len(GROUPS),)),
            dma((len(GROUPS),)),
            dma((len(GROUPS),)),
            dma((2, 5)),
            dma((2, 5)),
            dma,
        ],
        compiler_params=pltpu.CompilerParams(
            collective_id=0, has_side_effects=True, vmem_limit_bytes=60 << 20
        ),
        name="transport",
    )(
        owner_counts,
        adjoint_state.reshape(TR * LEV * CLAT, LANES),
        courant_east.reshape(LEV * CLAT, LANES),
        courant_north.reshape(LEV * CLAT, LANES),
        diffusion, convective_flux, convection,
        sounding_forcing,
        sounding_column.reshape(listed // LANES, LANES),
        sounding_level.reshape(listed // LANES, LANES),
    )
    anywhere = pl.BlockSpec(memory_space=pl.ANY)
    out, flux = pl.pallas_call(
        finish_kernel,
        out_shape=(
            jax.ShapeDtypeStruct((TR * LEV * CLAT, LANES), F32),
            jax.ShapeDtypeStruct((TR * CLAT, LANES), F32),
        ),
        in_specs=[anywhere] * 2,
        out_specs=(anywhere, anywhere),
        scratch_shapes=[
            pltpu.VMEM((TR * LEV * CLAT, LANES), F32),
            pltpu.VMEM((TR * CLAT, LANES), F32),
            dma((2, COPIES + 1)),
        ],
        compiler_params=pltpu.CompilerParams(vmem_limit_bytes=60 << 20),
        name="finish",
    )(out, flux)
    return out.reshape(TR, LEV, CLAT, LANES), flux.reshape(TR, CLAT, LANES)


def solution(mesh):
    return jax.shard_map(
        local,
        mesh=mesh,
        in_specs=(
            P(None, None, "lat", "lon"),
            P(None, "lat", "lon"),
            P(None, "lat", "lon"),
            P("lat", "lon"),
            P("lat", "lon"),
            P(),
            P(("lat", "lon"), None),
            P(("lat", "lon")),
            P(("lat", "lon")),
            P(("lat", "lon"), None),
        ),
        out_specs=(P(None, None, "lat", "lon"), P(None, "lat", "lon")),
        check_vma=False,
    )
```
